32 devices in a mesh: dp: 4 (over y, core), tower: 8 (over z, x).
Axes of the slice: x: 2, y: 2, z: 4, core: 2. Of those that a mesh axis runs over, the one named last changes fastest.
Arguments:
- attn_out: bfloat16 [4096, 4096], P(('dp', 'tower')), may hold values from -0.375 to 0.375
- out_cot: bfloat16 [4096, 4096], P(('dp', 'tower')), may hold values from -6 to 6
- modality: int32 [4096], P(('dp', 'tower')), may hold values from 0 to 2, as said below
- group_modality: int32 [8], replicated, may hold values from 0 to 2, as said below
- o_weight: bfloat16 [32768, 4096], P('tower'), as said below
Outputs:
- attn_grad: bfloat16 [4096, 4096], P(('dp', 'tower'))
- weight_grad: bfloat16 [32768, 4096], P('tower', 'dp')
The draws below stay inside these ranges and needn't reach their ends.
Inputs may be any that keep to these rules, and one draw needn't show every extreme that they name: `group_modality`: every modality is served by at least one group. In each block of 128 tokens (one device's tokens), a modality served by k groups appears at most k * 24 times; in every block the modality served by the fewest groups (the lowest such id on a tie) appears exactly that often. `o_weight`: groups that serve the same modality hold equal rows.
All inputs are finite; a program needn't handle non-finite values.
Results may differ from the reference program's by a relative error of at most 0.014.
Values may be sent and summed in bfloat16 or wider, within the bound.
No kernel may reach another device: no remote copies, remote signals or barrier semaphores. Data moves between devices by JAX's collectives and lax.ppermute only.
A program may use at most 128 MiB of HBM per device.

```python
import math
import jax
import jax.numpy as jnp
from jax import lax

D = 4096
TOK_DEV = 128
NGROUP = 8
CAP = 24
TOKENS = 4096
N_DP = 4
N_TOWER = 8


def group_table(key):
    first_key = jax.random.fold_in(key, 11)
    second_key = jax.random.fold_in(key, 12)
    extra = jax.random.randint(first_key, (NGROUP - 3,), 0, 3, dtype=jnp.int32)
    listed = jnp.concatenate([jnp.arange(3, dtype=jnp.int32), extra])
    return jax.random.permutation(second_key, listed)


def draw_group_modality(key, part):
    return group_table(key)


def draw_modality(key, part):
    table = group_table(key)
    modal_ids = jnp.arange(3, dtype=jnp.int32)
    per_kind = jnp.sum((table[:, None] == modal_ids[None, :]).astype(jnp.int32), axis=0)
    fewest = jnp.argmin(per_kind).astype(jnp.int32)
    slot_total = NGROUP * CAP
    slot_ids = jnp.arange(slot_total, dtype=jnp.int32)
    slot_kind = table[slot_ids // CAP]
    forced = slot_kind == fewest
    block_count = TOKENS // TOK_DEV
    block_keys = jax.random.split(jax.random.fold_in(key, 13), block_count)

    def one_block(block_key):
        score_key, order_key = jax.random.split(block_key)
        scores = jax.random.randint(score_key, (slot_total,), 0, 65536, dtype=jnp.int32) * slot_total + slot_ids
        scores = jnp.where(forced, 1073741824 + slot_ids, scores)
        _, picked = lax.top_k(scores, TOK_DEV)
        return jax.random.permutation(order_key, slot_kind[picked])
    return jax.vmap(one_block)(block_keys).reshape(-1).astype(jnp.int32)


def draw_o_weight(key, part):
    table = group_table(key)
    weight_key = jax.random.fold_in(key, 21)
    towers = jax.random.normal(weight_key, (3, D, D), jnp.float32) / math.sqrt(D)
    return towers[table].reshape(NGROUP * D, D).astype(jnp.bfloat16)


def level_of(own_key, shape, pieces, low, high):
    gain, own = 1.0, jax.random.fold_in(own_key, 6)
    for dim, blocks in pieces:
        steps = jnp.exp(jax.random.uniform(jax.random.fold_in(own, dim), (blocks,), jnp.float32, low / len(pieces), high / len(pieces)))
        gain = gain * jnp.repeat(steps, shape[dim] // blocks).reshape([-1 if axis == dim else 1 for axis in range(len(shape))])
    return gain


def scatter_about(key, shape, deviation, limit, pieces=(), kind=jnp.bfloat16):
    result = jax.random.normal(key, shape, jnp.float32) * deviation
    if len(pieces) > 0:
        result = level_of(key, shape, pieces, -0.22, 0.18) * result
    return jnp.clip(result, min=-limit, max=limit).astype(kind)


def setup_inputs(seed: int = 0) -> dict:
    key_of = jax.random.split(jax.random.key(seed), 6)
    attn_out = scatter_about(key_of[0], (TOKENS, D), 0.0625, 0.375, ((0, 32),))
    out_cot = scatter_about(key_of[1], (TOKENS, D), 1.0, 6.0, ((0, 32),))
    modality = draw_modality(jax.random.fold_in(key_of[5], 71), 0)
    group_modality = draw_group_modality(jax.random.fold_in(key_of[5], 71), 0)
    o_weight = draw_o_weight(jax.random.fold_in(key_of[5], 71), 0)
    return {"attn_out": attn_out, "out_cot": out_cot, "modality": modality, "group_modality": group_modality, "o_weight": o_weight}


def routing(modal_rows, tower_idx, group_modality):
    modal_ids = jnp.arange(3, dtype=jnp.int32)
    member = (modal_rows[:, None] == modal_ids[None, :]).astype(jnp.int32)
    before = jnp.cumsum(member, axis=0) - member
    order_in = jnp.sum(before * member, axis=1)
    group_of = (group_modality[:, None] == modal_ids[None, :]).astype(jnp.int32)
    per_kind = jnp.sum(group_of, axis=0)
    group_rank = jnp.sum((jnp.cumsum(group_of, axis=0) - group_of) * group_of, axis=1)
    how_many = jnp.sum(member * per_kind[None, :], axis=1)
    target = (order_in + tower_idx) % how_many
    chosen = (group_modality[None, :] == modal_rows[:, None]) & (group_rank[None, :] == target[:, None])
    group_ids = jnp.arange(group_modality.shape[0], dtype=jnp.int32)
    routed = jnp.sum(chosen.astype(jnp.int32) * group_ids[None, :], axis=1)
    slot_idx = order_in // how_many
    return routed, slot_idx


def reference(attn_out, out_cot, modality, group_modality, o_weight):
    blocks = N_DP * N_TOWER
    modal_rows = modality.reshape(blocks, TOK_DEV)
    towers = jnp.arange(blocks, dtype=jnp.int32) % N_TOWER
    routed, slot_idx = jax.vmap(routing, in_axes=(0, 0, None))(modal_rows, towers, group_modality)
    rows_per = N_TOWER * TOK_DEV
    slots_all = NGROUP * N_TOWER * CAP
    source = jnp.arange(N_TOWER, dtype=jnp.int32)[:, None]
    totals_init = jnp.zeros((NGROUP * D, D), jnp.float32)

    def row_step(totals, row_idx):
        route_row = lax.dynamic_slice_in_dim(routed, row_idx * N_TOWER, N_TOWER, 0)
        slot_row = lax.dynamic_slice_in_dim(slot_idx, row_idx * N_TOWER, N_TOWER, 0)
        landing = ((route_row * N_TOWER + source) * CAP + slot_row).reshape(-1).astype(jnp.int32)
        slot_table = jnp.full((slots_all,), rows_per, jnp.int32).at[landing].set(jnp.arange(rows_per, dtype=jnp.int32))
        slot_table = slot_table.reshape(NGROUP, N_TOWER * CAP)
        attn_row = lax.dynamic_slice_in_dim(attn_out, row_idx * rows_per, rows_per, 0)
        cot_row = lax.dynamic_slice_in_dim(out_cot, row_idx * rows_per, rows_per, 0)
        attn_pad = jnp.concatenate([attn_row, jnp.zeros((1, D), attn_row.dtype)], axis=0)
        cot_pad = jnp.concatenate([cot_row, jnp.zeros((1, D), cot_row.dtype)], axis=0)

        def group_step(carried, group_idx):
            grad_rows, totals_now = carried
            take_rows = slot_table[group_idx]
            attn_buf = attn_pad[take_rows]
            cot_buf = cot_pad[take_rows]
            weight = lax.dynamic_slice_in_dim(o_weight, group_idx * D, D, 0)
            grads = jnp.dot(cot_buf, weight.T, preferred_element_type=jnp.float32).astype(jnp.bfloat16)
            grad_rows = grad_rows.at[take_rows].set(grads, mode="drop")
            partial_value = jnp.dot(attn_buf.T, cot_buf, preferred_element_type=jnp.float32).astype(jnp.bfloat16)
            current = lax.dynamic_slice_in_dim(totals_now, group_idx * D, D, 0)
            totals_now = lax.dynamic_update_slice_in_dim(totals_now, current + partial_value.astype(jnp.float32), group_idx * D, 0)
            return (grad_rows, totals_now), None

        grad_init = jnp.zeros((rows_per, D), jnp.bfloat16)
        (grad_rows, totals), _ = lax.scan(group_step, (grad_init, totals), jnp.arange(NGROUP, dtype=jnp.int32))
        return totals, grad_rows

    totals, grad_all = lax.scan(row_step, totals_init, jnp.arange(N_DP, dtype=jnp.int32))
    return grad_all.reshape(TOKENS, D), totals.astype(jnp.bfloat16)
```

```python
import jax
import jax.numpy as jnp
from jax import lax
from jax.experimental import pallas as pl
from jax.experimental.pallas import tpu as pltpu
from jax.sharding import PartitionSpec as P

NGROUP = 8
CAP = 24
BF16 = jnp.bfloat16
F32 = jnp.float32


def routing(modal_rows, tower_idx, group_modality):
    modal_ids = jnp.arange(3, dtype=jnp.int32)
    member = (modal_rows[:, None] == modal_ids[None, :]).astype(jnp.int32)
    before = jnp.cumsum(member, axis=0) - member
    order_in = jnp.sum(before * member, axis=1)
    group_of = (group_modality[:, None] == modal_ids[None, :]).astype(jnp.int32)
    per_kind = jnp.sum(group_of, axis=0)
    group_rank = jnp.sum((jnp.cumsum(group_of, axis=0) - group_of) * group_of, axis=1)
    how_many = jnp.sum(member * per_kind[None, :], axis=1)
    target = (order_in + tower_idx) % how_many
    chosen = (group_modality[None, :] == modal_rows[:, None]) & (
        group_rank[None, :] == target[:, None]
    )
    group_ids = jnp.arange(group_modality.shape[0], dtype=jnp.int32)
    routed = jnp.sum(chosen.astype(jnp.int32) * group_ids[None, :], axis=1)
    slot_idx = order_in // how_many
    return (routed, slot_idx)


def weight_grad_kernel(count, *refs):
    attn_refs, cot_refs, out_ref = refs[:count], refs[count : 2 * count], refs[2 * count]
    total = None
    for attn_ref, cot_ref in zip(attn_refs, cot_refs):
        term = lax.dot_general(
            attn_ref[...], cot_ref[...], (((0,), (0,)), ((), ())), preferred_element_type=F32
        )
        total = term if total is None else total + term
    out_ref[...] = total.astype(out_ref.dtype)


def weight_grad_of(attn_parts, cot_parts):
    count = len(attn_parts)
    rows, features = attn_parts[0].shape
    columns = cot_parts[0].shape[1]
    block = min(512, features)
    return pl.pallas_call(
        lambda *refs: weight_grad_kernel(count, *refs),
        grid=(features // block,),
        in_specs=[pl.BlockSpec((rows, block), lambda i: (0, i))] * count
        + [pl.BlockSpec((rows, columns), lambda i: (0, 0))] * count,
        out_specs=pl.BlockSpec((block, columns), lambda i: (i, 0)),
        out_shape=jax.ShapeDtypeStruct((features, columns), BF16),
        cost_estimate=pl.CostEstimate(
            flops=2 * count * rows * features * columns,
            bytes_accessed=2 * (count * rows * (features + columns) + features * columns),
            transcendentals=0,
        ),
    )(*attn_parts, *cot_parts)


def per_device(attn_out, out_cot, modality, group_modality, o_weight):
    tower_idx = lax.axis_index("tower")
    tower_count = lax.axis_size("tower")
    dp_idx = lax.axis_index("dp")
    dp_count = lax.axis_size("dp")
    group_size = tower_count // NGROUP
    piece_rows = o_weight.shape[0]
    tok_count, model_width = attn_out.shape
    slot_rows = tower_count * CAP
    piece_cols = model_width // dp_count
    routed, slot_idx = routing(modality, tower_idx, group_modality)
    place = routed * CAP + slot_idx
    slots = jnp.arange(NGROUP * CAP, dtype=jnp.int32)
    dispatch = (place[None, :] == slots[:, None]).astype(BF16)

    cot_group = jnp.dot(dispatch, out_cot, preferred_element_type=F32).astype(BF16)
    attn_group = jnp.dot(dispatch, attn_out, preferred_element_type=F32).astype(BF16)
    cot_send = jnp.broadcast_to(
        cot_group.reshape(NGROUP, 1, CAP, model_width), (NGROUP, group_size, CAP, model_width)
    ).reshape(tower_count, CAP, model_width)
    attn_send = (
        attn_group.reshape(NGROUP, CAP, group_size, piece_rows)
        .transpose(0, 2, 1, 3)
        .reshape(tower_count, CAP, piece_rows)
    )
    cot_got = lax.all_to_all(cot_send, "tower", split_axis=0, concat_axis=0, tiled=True)
    attn_got = lax.all_to_all(attn_send, "tower", split_axis=0, concat_axis=0, tiled=True)
    cot_rows = cot_got.reshape(slot_rows, model_width)
    attn_rows = attn_got.reshape(slot_rows, piece_rows)

    grad_piece = lax.dot_general(
        cot_rows, o_weight, (((1,), (1,)), ((), ())), preferred_element_type=F32
    ).astype(BF16)
    returned = lax.all_to_all(
        grad_piece.reshape(tower_count, CAP, piece_rows), "tower", split_axis=0, concat_axis=0, tiled=True
    )
    returned = (
        returned.reshape(NGROUP, group_size, CAP, piece_rows)
        .transpose(0, 2, 1, 3)
        .reshape(NGROUP * CAP, model_width)
    )
    attn_grad = lax.dot_general(
        dispatch, returned, (((0,), (0,)), ((), ())), preferred_element_type=F32
    ).astype(BF16)

    def pairs(flip):
        return [(d, d ^ flip) for d in range(dp_count)]

    cot_parts = []
    for flip in range(dp_count):
        part = lax.dynamic_slice_in_dim(cot_rows, (dp_idx ^ flip) * piece_cols, piece_cols, 1)
        cot_parts.append(lax.ppermute(part, "dp", pairs(flip)) if flip else part)
    attn_parts = {0: attn_rows}
    flip = dp_count // 2
    while flip:
        for known in list(attn_parts):
            attn_parts[known ^ flip] = lax.ppermute(attn_parts[known], "dp", pairs(flip))
        flip //= 2
    weight_grad = weight_grad_of([attn_parts[flip] for flip in range(dp_count)], cot_parts)
    return (attn_grad, weight_grad)


def solution(mesh):
    return jax.shard_map(
        per_device,
        mesh=mesh,
        in_specs=(
            P(("dp", "tower"), None),
            P(("dp", "tower"), None),
            P(("dp", "tower")),
            P(),
            P("tower", None),
        ),
        out_specs=(P(("dp", "tower"), None), P("tower", "dp")),
        check_vma=False,
    )
```

```python
import functools

import jax
import jax.numpy as jnp
from jax import lax
from jax.experimental import pallas as pl
from jax.experimental.pallas import tpu as pltpu
from jax.sharding import PartitionSpec as P


NGROUP = 8
KINDS = 3
CAP = 24
BF16 = jnp.bfloat16
F32 = jnp.float32
I32 = jnp.int32


MIB = 1 << 20


def grant(mib):
    return pltpu.CompilerParams(vmem_limit_bytes=mib * MIB)


def cost(flops, moved):
    return pl.CostEstimate(flops=flops, bytes_accessed=moved, transcendentals=0)


def dispatch_matrix(tower_idx, kinds_ref, modal_row):
    tokens = modal_row.shape[1]
    earlier = lax.broadcasted_iota(I32, (tokens, tokens), 0) < lax.broadcasted_iota(
        I32, (tokens, tokens), 1
    )
    kind_rows = lax.broadcasted_iota(I32, (8, tokens), 0)
    member = jnp.where(kind_rows == modal_row, 1.0, 0.0)
    before = jnp.dot(
        member.astype(BF16),
        jnp.where(earlier, 1.0, 0.0).astype(BF16),
        preferred_element_type=F32,
    )
    order_in = jnp.sum(member * before, axis=0, keepdims=True)
    kinds = [kinds_ref[g] for g in range(NGROUP)]
    seen = [jnp.int32(0)] * KINDS
    ranks = []
    for g in range(NGROUP):
        rank = jnp.int32(0)
        for m in range(KINDS):
            hit = kinds[g] == m
            rank = jnp.where(hit, seen[m], rank)
            seen[m] = seen[m] + jnp.where(hit, 1, 0)
        ranks.append(rank)
    how_many = jnp.zeros((1, tokens), F32)
    for m in range(KINDS):
        how_many = jnp.where(modal_row == m, seen[m].astype(F32), how_many)
    inverse = 1.0 / jnp.maximum(how_many, 1.0)
    slot_idx = jnp.floor((order_in + 0.5) * inverse)
    shifted = order_in + tower_idx.astype(F32)
    target = shifted - how_many * jnp.floor((shifted + 0.5) * inverse)
    target = target.astype(I32)
    block = jnp.zeros((1, tokens), I32)
    for g in range(NGROUP):
        chosen = (modal_row == kinds[g]) & (target == ranks[g])
        block = jnp.where(chosen, jnp.bitwise_xor(jnp.int32(g), tower_idx), block)
    place = block * CAP + slot_idx.astype(I32)
    slots = lax.broadcasted_iota(I32, (NGROUP * CAP, tokens), 0)
    return jnp.where(slots == place, 1.0, 0.0).astype(BF16)


def first_dispatch_kernel(tower_ref, kinds_ref, modal_ref, rows_ref, one_hot_ref, *out_refs):
    @pl.when(pl.program_id(0) == 0)
    def _():
        one_hot_ref[...] = dispatch_matrix(tower_ref[0], kinds_ref, modal_ref[...])

    dispatch_kernel(one_hot_ref, rows_ref, *out_refs)


def dispatch_kernel(one_hot_ref, rows_ref, *out_refs):
    placed = jnp.dot(one_hot_ref[...], rows_ref[...], preferred_element_type=F32)
    for k, out_ref in enumerate(out_refs):
        out_ref[...] = placed[k * CAP : (k + 1) * CAP, :].astype(BF16)


def dispatch_first(tower_idx, kinds, modal_row, rows):
    tokens, width = rows.shape
    block = min(1024, width)
    slots = NGROUP * CAP
    out = pl.pallas_call(
        first_dispatch_kernel,
        grid=(width // block,),
        in_specs=[
            pl.BlockSpec(memory_space=pltpu.SMEM),
            pl.BlockSpec(memory_space=pltpu.SMEM),
            pl.BlockSpec((1, tokens), lambda i: (0, 0)),
            pl.BlockSpec((tokens, block), lambda i: (0, i)),
        ],
        out_specs=[pl.BlockSpec((slots, tokens), lambda i: (0, 0))]
        + [pl.BlockSpec((CAP, block), lambda i: (0, i))] * NGROUP,
        out_shape=[jax.ShapeDtypeStruct((slots, tokens), BF16)]
        + [jax.ShapeDtypeStruct((CAP, width), BF16)] * NGROUP,
        cost_estimate=cost(2 * slots * tokens * width, 2 * (tokens + slots) * width),
        compiler_params=grant(56),
        name="dispatch_cot",
    )(tower_idx, kinds, modal_row, rows)
    return out[0], list(out[1:])


def dispatch_next(one_hot, rows):
    tokens, width = rows.shape
    block = min(1024, width)
    slots = one_hot.shape[0]
    return list(
        pl.pallas_call(
            dispatch_kernel,
            grid=(width // block,),
            in_specs=[
                pl.BlockSpec((slots, tokens), lambda i: (0, 0)),
                pl.BlockSpec((tokens, block), lambda i: (0, i)),
            ],
            out_specs=[pl.BlockSpec((CAP, block), lambda i: (0, i))] * NGROUP,
            out_shape=[jax.ShapeDtypeStruct((CAP, width), BF16)] * NGROUP,
            cost_estimate=cost(2 * slots * tokens * width, 2 * (tokens + slots) * width),
            compiler_params=grant(12),
            name="dispatch_attn",
        )(one_hot, rows)
    )


def pieces_kernel(dp_ref, *refs):
    block_refs, out_refs = refs[:NGROUP], refs[NGROUP:]
    columns = out_refs[0].shape[1]
    for f, out_ref in enumerate(out_refs):
        first = pl.multiple_of(jnp.bitwise_xor(dp_ref[0], jnp.int32(f)) * columns, 128)
        for k, block_ref in enumerate(block_refs):
            out_ref[k * CAP : (k + 1) * CAP, :] = block_ref[:, pl.ds(first, columns)]


def column_pieces(dp_idx, blocks):
    pieces = lax.axis_size("dp")
    width = blocks[0].shape[1]
    slots = NGROUP * CAP
    whole = pl.BlockSpec(memory_space=pltpu.VMEM)
    return pl.pallas_call(
        pieces_kernel,
        in_specs=[pl.BlockSpec(memory_space=pltpu.SMEM)] + [whole] * NGROUP,
        out_specs=[whole] * pieces,
        out_shape=[jax.ShapeDtypeStruct((slots, width // pieces), BF16)] * pieces,
        cost_estimate=cost(0, 4 * slots * width),
        compiler_params=grant(8),
        name="column_pieces",
    )(dp_idx, *blocks)


def token_grad_kernel(pieces, dp_ref, *refs):
    cot_refs, weight_refs, out_refs = refs[:pieces], refs[pieces : 2 * pieces], refs[2 * pieces :]
    grads = None
    for cot_ref, weight_ref in zip(cot_refs, weight_refs):
        term = lax.dot_general(
            cot_ref[...], weight_ref[...], (((1,), (1,)), ((), ())), preferred_element_type=F32
        )
        grads = term if grads is None else grads + term
    for k, out_ref in enumerate(out_refs):
        out_ref[...] = grads[k * CAP : (k + 1) * CAP, :].astype(BF16)


def token_grad(dp_idx, cot_pieces, weight):
    features, width = weight.shape
    pieces = len(cot_pieces)
    slots, columns = cot_pieces[0].shape
    block = min(512, features)

    def weight_spec(f):
        return pl.BlockSpec((block, columns), lambda i, dp_ref: (i, jnp.bitwise_xor(dp_ref[0], f)))

    return list(
        pl.pallas_call(
            functools.partial(token_grad_kernel, pieces),
            grid_spec=pltpu.PrefetchScalarGridSpec(
                num_scalar_prefetch=1,
                grid=(features // block,),
                in_specs=[pl.BlockSpec((slots, columns), lambda i, dp_ref: (0, 0))] * pieces
                + [weight_spec(f) for f in range(pieces)],
                out_specs=[pl.BlockSpec((CAP, block), lambda i, dp_ref: (0, i))] * NGROUP,
            ),
            out_shape=[jax.ShapeDtypeStruct((CAP, features), BF16)] * NGROUP,
            cost_estimate=cost(
                2 * slots * features * width, 2 * (features * width + 2 * slots * width)
            ),
            compiler_params=grant(20),
            name="token_grad",
        )(dp_idx, *cot_pieces, *[weight] * pieces)
    )


def combine_kernel(one_hot_ref, *refs):
    got_refs, out_ref, rows_ref = refs[:NGROUP], refs[NGROUP], refs[NGROUP + 1]
    for k, got_ref in enumerate(got_refs):
        rows_ref[k * CAP : (k + 1) * CAP, :] = got_ref[...]
    out_ref[...] = lax.dot_general(
        one_hot_ref[...], rows_ref[...], (((0,), (0,)), ((), ())), preferred_element_type=F32
    ).astype(BF16)


def combine(one_hot, blocks):
    slots, tokens = one_hot.shape
    width = blocks[0].shape[1]
    block = min(1024, width)
    return pl.pallas_call(
        combine_kernel,
        grid=(width // block,),
        in_specs=[pl.BlockSpec((slots, tokens), lambda i: (0, 0))]
        + [pl.BlockSpec((CAP, block), lambda i: (0, i))] * NGROUP,
        out_specs=pl.BlockSpec((tokens, block), lambda i: (0, i)),
        out_shape=jax.ShapeDtypeStruct((tokens, width), BF16),
        scratch_shapes=[pltpu.VMEM((slots, block), BF16)],
        cost_estimate=cost(2 * slots * tokens * width, 2 * (tokens + slots) * width),
        compiler_params=grant(8),
        name="combine",
    )(one_hot, *blocks)


def join_kernel(*refs):
    at = 0
    for ref in refs[:-1]:
        rows = ref.shape[0]
        refs[-1][at : at + rows, :] = ref[...]
        at += rows


def join_rows(blocks):
    rows = sum(block.shape[0] for block in blocks)
    width = blocks[0].shape[1]
    whole = pl.BlockSpec(memory_space=pltpu.VMEM)
    return pl.pallas_call(
        join_kernel,
        in_specs=[whole] * len(blocks),
        out_specs=whole,
        out_shape=jax.ShapeDtypeStruct((rows, width), BF16),
        cost_estimate=cost(0, 4 * rows * width),
        compiler_params=grant(8),
        name="join_rows",
    )(*blocks)


def weight_grad_kernel(n_attn, n_cot, *refs):
    attn_refs, cot_refs = refs[:n_attn], refs[n_attn : n_attn + n_cot]
    out_ref, attn_rows_ref, cot_rows_ref = refs[n_attn + n_cot :]

    @pl.when(pl.program_id(0) == 0)
    def _():
        at = 0
        for cot_ref in cot_refs:
            rows = cot_ref.shape[0]
            cot_rows_ref[at : at + rows, :] = cot_ref[...]
            at += rows

    at = 0
    for attn_ref in attn_refs:
        rows = attn_ref.shape[0]
        attn_rows_ref[at : at + rows, :] = attn_ref[...]
        at += rows
    out_ref[...] = lax.dot_general(
        attn_rows_ref[...],
        cot_rows_ref[...],
        (((0,), (0,)), ((), ())),
        preferred_element_type=F32,
    ).astype(out_ref.dtype)


def weight_grad_of(attn_parts, cot_parts):
    features = attn_parts[0].shape[1]
    columns = cot_parts[0].shape[1]
    rows = sum(part.shape[0] for part in attn_parts)
    block = min(512, features)
    return pl.pallas_call(
        functools.partial(weight_grad_kernel, len(attn_parts), len(cot_parts)),
        grid=(features // block,),
        in_specs=[pl.BlockSpec((part.shape[0], block), lambda i: (0, i)) for part in attn_parts]
        + [pl.BlockSpec((part.shape[0], columns), lambda i: (0, 0)) for part in cot_parts],
        out_specs=pl.BlockSpec((block, columns), lambda i: (i, 0)),
        out_shape=jax.ShapeDtypeStruct((features, columns), BF16),
        scratch_shapes=[pltpu.VMEM((rows, block), BF16), pltpu.VMEM((rows, columns), BF16)],
        cost_estimate=cost(
            2 * rows * features * columns, 2 * (rows * (features + columns) + features * columns)
        ),
        compiler_params=grant(20),
        name="weight_grad",
    )(*attn_parts, *cot_parts)


def flip_over(axis, value, flip):
    size = lax.axis_size(axis)
    return lax.ppermute(value, axis, [(i, i ^ flip) for i in range(size)])


def swap_blocks(blocks, order):
    got = {0: blocks[0]}
    for k in order:
        got[k] = flip_over("tower", blocks[k], k)
    return [got[k] for k in range(len(blocks))]


def gather_flips(value):
    parts = {0: value}
    flip = lax.axis_size("dp") // 2
    while flip:
        for known in list(parts):
            parts[known ^ flip] = flip_over("dp", parts[known], flip)
        flip //= 2
    return parts


FAR = (6, 7, 4, 5)
NEAR = (2, 3, 1)
LOWER = (0, 1, 2, 3)
UPPER = (4, 5, 6, 7)


def small_towers(attn_out, out_cot, modality, group_modality, o_weight):
    tower_idx = lax.axis_index("tower").astype(I32)
    dp_idx = lax.axis_index("dp").astype(I32).reshape(1)
    dp_count = lax.axis_size("dp")

    one_hot, cot_blocks = dispatch_first(
        tower_idx.reshape(1), group_modality, modality.reshape(1, -1), out_cot
    )
    attn_blocks = dispatch_next(one_hot, attn_out)
    cot_got = swap_blocks(cot_blocks, FAR + NEAR)
    attn_got = swap_blocks(attn_blocks, NEAR + FAR)
    cot_pieces = column_pieces(dp_idx, cot_got)
    cot_parts = [
        flip_over("dp", piece, flip) if flip else piece
        for flip, piece in enumerate(cot_pieces)
    ]
    grads = token_grad(dp_idx, cot_pieces, o_weight)
    returned = swap_blocks(grads, FAR + NEAR)
    attn_grad = combine(one_hot, returned)

    lower = join_rows([attn_got[k] for k in LOWER])
    upper = join_rows([attn_got[k] for k in UPPER])
    lower = gather_flips(lower)
    upper = gather_flips(upper)
    attn_parts = []
    for flip in range(dp_count):
        attn_parts += [lower[flip], upper[flip]]
    return attn_grad, weight_grad_of(attn_parts, cot_parts)


def large_towers(attn_out, out_cot, modality, group_modality, o_weight):
    tower_idx = lax.axis_index("tower").astype(I32)
    tower_count = lax.axis_size("tower")
    dp_idx = lax.axis_index("dp")
    dp_count = lax.axis_size("dp")
    group_size = tower_count // NGROUP
    piece_rows, width = o_weight.shape
    tokens = attn_out.shape[0]
    piece_cols = width // dp_count
    modal_row = modality.reshape(1, tokens)
    group_ids = jnp.arange(NGROUP, dtype=I32)
    member = modal_row == jnp.arange(KINDS, dtype=I32)[:, None]
    before = jnp.cumsum(member.astype(I32), axis=1) - 1
    order_in = jnp.sum(jnp.where(member, before, 0), axis=0)
    group_of = (group_modality[:, None] == jnp.arange(KINDS, dtype=I32)[None, :]).astype(I32)
    group_rank = jnp.sum((jnp.cumsum(group_of, axis=0) - group_of) * group_of, axis=1)
    how_many = jnp.sum(member * jnp.sum(group_of, axis=0)[:, None], axis=0)
    target = (order_in + tower_idx) % how_many
    chosen = (group_modality[:, None] == modal_row) & (group_rank[:, None] == target[None, :])
    routed = jnp.sum(chosen.astype(I32) * group_ids[:, None], axis=0)
    place = routed * CAP + order_in // how_many
    one_hot = (place[None, :] == jnp.arange(NGROUP * CAP, dtype=I32)[:, None]).astype(BF16)

    def swap(value):
        return lax.all_to_all(value, "tower", split_axis=0, concat_axis=0, tiled=True)

    cot_group = jnp.dot(one_hot, out_cot, preferred_element_type=F32).astype(BF16)
    attn_group = jnp.dot(one_hot, attn_out, preferred_element_type=F32).astype(BF16)
    cot_send = jnp.broadcast_to(
        cot_group.reshape(NGROUP, 1, CAP, width), (NGROUP, group_size, CAP, width)
    ).reshape(tower_count, CAP, width)
    attn_send = (
        attn_group.reshape(NGROUP, CAP, group_size, piece_rows)
        .transpose(0, 2, 1, 3)
        .reshape(tower_count, CAP, piece_rows)
    )
    cot_rows = swap(cot_send).reshape(tower_count * CAP, width)
    attn_rows = swap(attn_send).reshape(tower_count * CAP, piece_rows)
    grads = lax.dot_general(
        cot_rows, o_weight, (((1,), (1,)), ((), ())), preferred_element_type=F32
    ).astype(BF16)
    returned = (
        swap(grads.reshape(tower_count, CAP, piece_rows))
        .reshape(NGROUP, group_size, CAP, piece_rows)
        .transpose(0, 2, 1, 3)
        .reshape(NGROUP * CAP, width)
    )
    attn_grad = lax.dot_general(
        one_hot, returned, (((0,), (0,)), ((), ())), preferred_element_type=F32
    ).astype(BF16)
    cot_parts = []
    for flip in range(dp_count):
        part = lax.dynamic_slice_in_dim(cot_rows, (dp_idx ^ flip) * piece_cols, piece_cols, 1)
        cot_parts.append(flip_over("dp", part, flip) if flip else part)
    attn_parts = gather_flips(attn_rows)
    return attn_grad, weight_grad_of([attn_parts[flip] for flip in range(dp_count)], cot_parts)


def per_device(*args):
    if lax.axis_size("tower") == NGROUP:
        return small_towers(*args)
    return large_towers(*args)


def solution(mesh):
    return jax.shard_map(
        per_device,
        mesh=mesh,
        in_specs=(
            P(("dp", "tower"), None),
            P(("dp", "tower"), None),
            P(("dp", "tower")),
            P(),
            P("tower", None),
        ),
        out_specs=(P(("dp", "tower"), None), P("tower", "dp")),
        check_vma=False,
    )
```

```python
import functools

import jax
import jax.numpy as jnp
from jax import lax
from jax.experimental import pallas as pl
from jax.experimental.pallas import tpu as pltpu
from jax.sharding import PartitionSpec as P


NGROUP = 8
KINDS = 3
CAP = 24
BF16 = jnp.bfloat16
F32 = jnp.float32
I32 = jnp.int32


MIB = 1 << 20


def grant(mib):
    return pltpu.CompilerParams(vmem_limit_bytes=mib * MIB)


def cost(flops, moved):
    return pl.CostEstimate(flops=flops, bytes_accessed=moved, transcendentals=0)


RING = NGROUP // 2
STEPS = (0, 1, 3, 2)


def block_to(group, tower_idx):
    steps = (group // 2 - jnp.right_shift(tower_idx, 1)) & (RING - 1)
    place = jnp.int32(0)
    for at, step in enumerate(STEPS):
        place = jnp.where(steps == step, at, place)
    return place * 2 + ((group & 1) ^ (tower_idx & 1))


def target_of(tower_idx, block):
    return (tower_idx // 2 + STEPS[block // 2]) % RING * 2 + (tower_idx + block) % 2


def dispatch_matrix(tower_idx, kinds_ref, modal_row):
    tokens = modal_row.shape[1]
    earlier = lax.broadcasted_iota(I32, (tokens, tokens), 0) < lax.broadcasted_iota(
        I32, (tokens, tokens), 1
    )
    kind_rows = lax.broadcasted_iota(I32, (8, tokens), 0)
    member = jnp.where(kind_rows == modal_row, 1.0, 0.0)
    before = jnp.dot(
        member.astype(BF16),
        jnp.where(earlier, 1.0, 0.0).astype(BF16),
        preferred_element_type=F32,
    )
    order_in = jnp.sum(member * before, axis=0, keepdims=True)
    kinds = [kinds_ref[g] for g in range(NGROUP)]
    seen = [jnp.int32(0)] * KINDS
    ranks = []
    for g in range(NGROUP):
        rank = jnp.int32(0)
        for m in range(KINDS):
            hit = kinds[g] == m
            rank = jnp.where(hit, seen[m], rank)
            seen[m] = seen[m] + jnp.where(hit, 1, 0)
        ranks.append(rank)
    how_many = jnp.zeros((1, tokens), F32)
    for m in range(KINDS):
        how_many = jnp.where(modal_row == m, seen[m].astype(F32), how_many)
    inverse = 1.0 / jnp.maximum(how_many, 1.0)
    slot_idx = jnp.floor((order_in + 0.5) * inverse)
    shifted = order_in + tower_idx.astype(F32)
    target = shifted - how_many * jnp.floor((shifted + 0.5) * inverse)
    target = target.astype(I32)
    block = jnp.zeros((1, tokens), I32)
    for g in range(NGROUP):
        chosen = (modal_row == kinds[g]) & (target == ranks[g])
        block = jnp.where(chosen, block_to(g, tower_idx), block)
    place = block * CAP + slot_idx.astype(I32)
    slots = lax.broadcasted_iota(I32, (NGROUP * CAP, tokens), 0)
    return jnp.where(slots == place, 1.0, 0.0).astype(BF16)


def first_dispatch_kernel(chunks, tower_ref, kinds_hbm, modal_hbm, rows_hbm, one_hot_ref, *refs):
    out_refs, (kinds_ref, modal_ref, rows_ref, known, arrived) = refs[:NGROUP], refs[NGROUP:]
    width = rows_ref.shape[1] // chunks
    tables = [
        pltpu.make_async_copy(kinds_hbm, kinds_ref, known.at[0]),
        pltpu.make_async_copy(modal_hbm, modal_ref, known.at[1]),
    ]
    for table in tables:
        table.start()
    copies = []
    for c in range(chunks):
        columns = pl.ds(c * width, width)
        copies.append(
            pltpu.make_async_copy(rows_hbm.at[:, columns], rows_ref.at[:, columns], arrived.at[c])
        )
        copies[c].start()
    for table in tables:
        table.wait()
    one_hot_ref[...] = dispatch_matrix(tower_ref[0], kinds_ref, modal_ref[...])
    for c in range(chunks):
        columns = pl.ds(c * width, width)
        copies[c].wait()
        placed = jnp.dot(one_hot_ref[...], rows_ref[:, columns], preferred_element_type=F32)
        for k, out_ref in enumerate(out_refs):
            out_ref[:, columns] = placed[k * CAP : (k + 1) * CAP, :].astype(BF16)


def dispatch_kernel(one_hot_ref, rows_ref, *out_refs):
    placed = jnp.dot(one_hot_ref[...], rows_ref[...], preferred_element_type=F32)
    for k, out_ref in enumerate(out_refs):
        out_ref[...] = placed[k * CAP : (k + 1) * CAP, :].astype(BF16)


def dispatch_first(tower_idx, kinds, modal_row, rows):
    tokens, width = rows.shape
    chunks = 4
    slots = NGROUP * CAP
    in_smem = pl.BlockSpec(memory_space=pltpu.SMEM)
    in_vmem = pl.BlockSpec(memory_space=pltpu.VMEM)
    out = pl.pallas_call(
        functools.partial(first_dispatch_kernel, chunks),
        in_specs=[in_smem] + [pl.BlockSpec(memory_space=pltpu.HBM)] * 3,
        out_specs=[in_vmem] * (NGROUP + 1),
        out_shape=[jax.ShapeDtypeStruct((slots, tokens), BF16)]
        + [jax.ShapeDtypeStruct((CAP, width), BF16)] * NGROUP,
        scratch_shapes=[
            pltpu.SMEM((NGROUP,), I32),
            pltpu.VMEM((1, tokens), I32),
            pltpu.VMEM((tokens, width), BF16),
            pltpu.SemaphoreType.DMA((2,)),
            pltpu.SemaphoreType.DMA((chunks,)),
        ],
        cost_estimate=cost(2 * slots * tokens * width, 2 * (tokens + slots) * width),
        compiler_params=grant(56),
        name="dispatch_cot",
    )(tower_idx, kinds, modal_row, rows)
    return out[0], list(out[1:])


def dispatch_next(one_hot, rows):
    tokens, width = rows.shape
    block = min(1024, width)
    slots = one_hot.shape[0]
    return list(
        pl.pallas_call(
            dispatch_kernel,
            grid=(width // block,),
            in_specs=[
                pl.BlockSpec((slots, tokens), lambda i: (0, 0)),
                pl.BlockSpec((tokens, block), lambda i: (0, i)),
            ],
            out_specs=[pl.BlockSpec((CAP, block), lambda i: (0, i))] * NGROUP,
            out_shape=[jax.ShapeDtypeStruct((CAP, width), BF16)] * NGROUP,
            cost_estimate=cost(2 * slots * tokens * width, 2 * (tokens + slots) * width),
            compiler_params=grant(12),
            name="dispatch_attn",
        )(one_hot, rows)
    )


def pieces_kernel(count, dp_ref, *refs):
    block_refs, out_refs = refs[:count], refs[count:]
    columns = out_refs[0].shape[1]
    for f, out_ref in enumerate(out_refs):
        first = pl.multiple_of(jnp.bitwise_xor(dp_ref[0], jnp.int32(f)) * columns, 128)
        for k, block_ref in enumerate(block_refs):
            out_ref[k * CAP : (k + 1) * CAP, :] = block_ref[:, pl.ds(first, columns)]


def column_pieces(dp_idx, blocks):
    pieces = lax.axis_size("dp")
    width = blocks[0].shape[1]
    rows = len(blocks) * CAP
    whole = pl.BlockSpec(memory_space=pltpu.VMEM)
    return pl.pallas_call(
        functools.partial(pieces_kernel, len(blocks)),
        in_specs=[pl.BlockSpec(memory_space=pltpu.SMEM)] + [whole] * len(blocks),
        out_specs=[whole] * pieces,
        out_shape=[jax.ShapeDtypeStruct((rows, width // pieces), BF16)] * pieces,
        cost_estimate=cost(0, 4 * rows * width),
        compiler_params=grant(8),
        name="column_pieces",
    )(dp_idx, *blocks)


def token_grad_kernel(pieces, parts, dp_ref, *refs):
    cot_refs, weight_refs = refs[: pieces * parts], refs[pieces * parts : pieces * (parts + 1)]
    out_refs, rows_refs = refs[pieces * (parts + 1) : -pieces], refs[-pieces:]

    @pl.when(pl.program_id(0) == 0)
    def _():
        for f, rows_ref in enumerate(rows_refs):
            at = 0
            for cot_ref in cot_refs[f::pieces]:
                rows_ref[at : at + cot_ref.shape[0], :] = cot_ref[...]
                at += cot_ref.shape[0]

    grads = None
    for rows_ref, weight_ref in zip(rows_refs, weight_refs):
        term = lax.dot_general(
            rows_ref[...], weight_ref[...], (((1,), (1,)), ((), ())), preferred_element_type=F32
        )
        grads = term if grads is None else grads + term
    for k, out_ref in enumerate(out_refs):
        out_ref[...] = grads[k * CAP : (k + 1) * CAP, :].astype(BF16)


def token_grad(dp_idx, cot_pieces, weight):
    features, width = weight.shape
    pieces = len(cot_pieces[0])
    columns = width // pieces
    slots = NGROUP * CAP
    block = min(512, features)

    def weight_spec(f):
        return pl.BlockSpec((block, columns), lambda i, dp_ref: (i, jnp.bitwise_xor(dp_ref[0], f)))

    flat = [piece for part in cot_pieces for piece in part]
    return list(
        pl.pallas_call(
            functools.partial(token_grad_kernel, pieces, len(cot_pieces)),
            grid_spec=pltpu.PrefetchScalarGridSpec(
                num_scalar_prefetch=1,
                grid=(features // block,),
                in_specs=[pl.BlockSpec(piece.shape, lambda i, dp_ref: (0, 0)) for piece in flat]
                + [weight_spec(f) for f in range(pieces)],
                out_specs=[pl.BlockSpec((CAP, block), lambda i, dp_ref: (0, i))] * NGROUP,
                scratch_shapes=[pltpu.VMEM((slots, columns), BF16)] * pieces,
            ),
            out_shape=[jax.ShapeDtypeStruct((CAP, features), BF16)] * NGROUP,
            cost_estimate=cost(
                2 * slots * features * width, 2 * (features * width + 2 * slots * width)
            ),
            compiler_params=grant(24),
            name="token_grad",
        )(dp_idx, *flat, *[weight] * pieces)
    )


def rows_back(one_hot_ref, first, got_refs, rows_ref, columns):
    for k, got_ref in enumerate(got_refs):
        rows_ref[k * CAP : (k + 1) * CAP, columns] = got_ref[:, columns]
    return lax.dot_general(
        one_hot_ref[first * CAP : (first + len(got_refs)) * CAP, :],
        rows_ref[:, columns],
        (((0,), (0,)), ((), ())),
        preferred_element_type=F32,
    )


def combine_first_kernel(chunks, one_hot_ref, *refs):
    got_refs, out_ref, rows_ref = refs[:-2], refs[-2], refs[-1]
    width = out_ref.shape[1] // chunks
    for c in range(chunks):
        columns = pl.ds(c * width, width)
        out_ref[:, columns] = rows_back(one_hot_ref, 0, got_refs, rows_ref, columns).astype(BF16)


def combine_last_kernel(chunks, first, one_hot_ref, partial_ref, *refs):
    got_refs, out_hbm, rows_ref, out_ref, written = refs[:-4], *refs[-4:]
    width = out_ref.shape[1] // chunks
    copies = []
    for c in range(chunks):
        columns = pl.ds(c * width, width)
        total = rows_back(one_hot_ref, first, got_refs, rows_ref, columns)
        out_ref[:, columns] = (total + partial_ref[:, columns].astype(F32)).astype(BF16)
        copies.append(
            pltpu.make_async_copy(out_ref.at[:, columns], out_hbm.at[:, columns], written.at[c])
        )
        copies[c].start()
    for copy in copies:
        copy.wait()


def combine_first(one_hot, blocks):
    tokens = one_hot.shape[1]
    width = blocks[0].shape[1]
    rows = len(blocks) * CAP
    whole = pl.BlockSpec(memory_space=pltpu.VMEM)
    return pl.pallas_call(
        functools.partial(combine_first_kernel, 4),
        in_specs=[whole] * (1 + len(blocks)),
        out_specs=whole,
        out_shape=jax.ShapeDtypeStruct((tokens, width), BF16),
        scratch_shapes=[pltpu.VMEM((rows, width), BF16)],
        cost_estimate=cost(2 * rows * tokens * width, 2 * (tokens + rows) * width),
        compiler_params=grant(12),
        name="combine_first",
    )(one_hot, *blocks)


def combine_last(one_hot, partial, blocks):
    tokens, width = partial.shape
    chunks = 4
    rows = len(blocks) * CAP
    whole = pl.BlockSpec(memory_space=pltpu.VMEM)
    return pl.pallas_call(
        functools.partial(combine_last_kernel, chunks, NGROUP - len(blocks)),
        in_specs=[whole] * (2 + len(blocks)),
        out_specs=pl.BlockSpec(memory_space=pl.ANY),
        out_shape=jax.ShapeDtypeStruct((tokens, width), BF16),
        scratch_shapes=[
            pltpu.VMEM((rows, width), BF16),
            pltpu.VMEM((tokens, width), BF16),
            pltpu.SemaphoreType.DMA((chunks,)),
        ],
        cost_estimate=cost(2 * rows * tokens * width, 2 * (2 * tokens + rows) * width),
        compiler_params=grant(12),
        name="combine_last",
    )(one_hot, partial, *blocks)


def join_kernel(*refs):
    at = 0
    for ref in refs[:-1]:
        rows = ref.shape[0]
        refs[-1][at : at + rows, :] = ref[...]
        at += rows


def join_rows(blocks):
    if len(blocks) == 1:
        return blocks[0]
    rows = sum(block.shape[0] for block in blocks)
    width = blocks[0].shape[1]
    whole = pl.BlockSpec(memory_space=pltpu.VMEM)
    return pl.pallas_call(
        join_kernel,
        in_specs=[whole] * len(blocks),
        out_specs=whole,
        out_shape=jax.ShapeDtypeStruct((rows, width), BF16),
        cost_estimate=cost(0, 4 * rows * width),
        compiler_params=grant(8),
        name="join_rows",
    )(*blocks)


def weight_grad_kernel(n_attn, n_cot, *refs):
    attn_refs, cot_refs = refs[:n_attn], refs[n_attn : n_attn + n_cot]
    out_ref, attn_rows_ref, cot_rows_ref = refs[n_attn + n_cot :]

    @pl.when(pl.program_id(0) == 0)
    def _():
        at = 0
        for cot_ref in cot_refs:
            rows = cot_ref.shape[0]
            cot_rows_ref[at : at + rows, :] = cot_ref[...]
            at += rows

    at = 0
    for attn_ref in attn_refs:
        rows = attn_ref.shape[0]
        attn_rows_ref[at : at + rows, :] = attn_ref[...]
        at += rows
    out_ref[...] = lax.dot_general(
        attn_rows_ref[...],
        cot_rows_ref[...],
        (((0,), (0,)), ((), ())),
        preferred_element_type=F32,
    ).astype(out_ref.dtype)


def weight_grad_of(attn_parts, cot_parts):
    features = attn_parts[0].shape[1]
    columns = cot_parts[0].shape[1]
    rows = sum(part.shape[0] for part in attn_parts)
    block = min(512, features)
    return pl.pallas_call(
        functools.partial(weight_grad_kernel, len(attn_parts), len(cot_parts)),
        grid=(features // block,),
        in_specs=[pl.BlockSpec((part.shape[0], block), lambda i: (0, i)) for part in attn_parts]
        + [pl.BlockSpec((part.shape[0], columns), lambda i: (0, 0)) for part in cot_parts],
        out_specs=pl.BlockSpec((block, columns), lambda i: (i, 0)),
        out_shape=jax.ShapeDtypeStruct((features, columns), BF16),
        scratch_shapes=[pltpu.VMEM((rows, block), BF16), pltpu.VMEM((rows, columns), BF16)],
        cost_estimate=cost(
            2 * rows * features * columns, 2 * (rows * (features + columns) + features * columns)
        ),
        compiler_params=grant(20),
        name="weight_grad",
    )(*attn_parts, *cot_parts)


def flip_over(axis, value, flip):
    size = lax.axis_size(axis)
    return lax.ppermute(value, axis, [(i, i ^ flip) for i in range(size)])


def swap_blocks(blocks, back=False):
    got = [blocks[0]]
    for k in range(1, NGROUP):
        pairs = [(t, target_of(t, k)) for t in range(NGROUP)]
        if back:
            pairs = [(target, source) for source, target in pairs]
        got.append(lax.ppermute(blocks[k], "tower", pairs))
    return got


def gather_flips(value):
    parts = {0: value}
    flip = lax.axis_size("dp") // 2
    while flip:
        for known in list(parts):
            parts[known ^ flip] = flip_over("dp", parts[known], flip)
        flip //= 2
    return parts


COT_PARTS = {"cot_early": (0, 1, 2, 3), "cot_late": (4, 5, 6, 7)}
ATTN_PARTS = {"attn_a": (0, 1), "attn_b": (2,), "attn_c": (3, 4, 5), "attn_d": (6, 7)}
LAST = (6, 7)


def small_towers(attn_out, out_cot, modality, group_modality, o_weight):
    tower_idx = lax.axis_index("tower").astype(I32)
    dp_idx = lax.axis_index("dp").astype(I32).reshape(1)
    dp_count = lax.axis_size("dp")

    one_hot, cot_blocks = dispatch_first(
        tower_idx.reshape(1), group_modality, modality.reshape(1, -1), out_cot
    )
    attn_blocks = dispatch_next(one_hot, attn_out)
    cot_got = swap_blocks(cot_blocks)
    attn_got = swap_blocks(attn_blocks)
    cot_pieces, cot_moved = [], []
    for blocks in COT_PARTS.values():
        pieces = column_pieces(dp_idx, [cot_got[k] for k in blocks])
        cot_pieces.append(pieces)
        cot_moved.append(
            [flip_over("dp", piece, flip) if flip else piece for flip, piece in enumerate(pieces)]
        )
    cot_parts = [moved[flip] for flip in range(dp_count) for moved in cot_moved]
    grads = token_grad(dp_idx, cot_pieces, o_weight)
    returned = swap_blocks(grads, back=True)
    partial = combine_first(one_hot, [returned[k] for k in range(NGROUP) if k not in LAST])
    attn_grad = combine_last(one_hot, partial, [returned[k] for k in LAST])

    parts = []
    for blocks in ATTN_PARTS.values():
        joined = join_rows([attn_got[k] for k in blocks])
        parts.append(gather_flips(joined))
    attn_parts = [part[flip] for flip in range(dp_count) for part in parts]
    return attn_grad, weight_grad_of(attn_parts, cot_parts)


def large_towers(attn_out, out_cot, modality, group_modality, o_weight):
    tower_idx = lax.axis_index("tower").astype(I32)
    tower_count = lax.axis_size("tower")
    dp_idx = lax.axis_index("dp")
    dp_count = lax.axis_size("dp")
    group_size = tower_count // NGROUP
    piece_rows, width = o_weight.shape
    tokens = attn_out.shape[0]
    piece_cols = width // dp_count
    modal_row = modality.reshape(1, tokens)
    group_ids = jnp.arange(NGROUP, dtype=I32)
    member = modal_row == jnp.arange(KINDS, dtype=I32)[:, None]
    before = jnp.cumsum(member.astype(I32), axis=1) - 1
    order_in = jnp.sum(jnp.where(member, before, 0), axis=0)
    group_of = (group_modality[:, None] == jnp.arange(KINDS, dtype=I32)[None, :]).astype(I32)
    group_rank = jnp.sum((jnp.cumsum(group_of, axis=0) - group_of) * group_of, axis=1)
    how_many = jnp.sum(member * jnp.sum(group_of, axis=0)[:, None], axis=0)
    target = (order_in + tower_idx) % how_many
    chosen = (group_modality[:, None] == modal_row) & (group_rank[:, None] == target[None, :])
    routed = jnp.sum(chosen.astype(I32) * group_ids[:, None], axis=0)
    place = routed * CAP + order_in // how_many
    one_hot = (place[None, :] == jnp.arange(NGROUP * CAP, dtype=I32)[:, None]).astype(BF16)

    def swap(value):
        return lax.all_to_all(value, "tower", split_axis=0, concat_axis=0, tiled=True)

    cot_group = jnp.dot(one_hot, out_cot, preferred_element_type=F32).astype(BF16)
    attn_group = jnp.dot(one_hot, attn_out, preferred_element_type=F32).astype(BF16)
    cot_send = jnp.broadcast_to(
        cot_group.reshape(NGROUP, 1, CAP, width), (NGROUP, group_size, CAP, width)
    ).reshape(tower_count, CAP, width)
    attn_send = (
        attn_group.reshape(NGROUP, CAP, group_size, piece_rows)
        .transpose(0, 2, 1, 3)
        .reshape(tower_count, CAP, piece_rows)
    )
    cot_rows = swap(cot_send).reshape(tower_count * CAP, width)
    attn_rows = swap(attn_send).reshape(tower_count * CAP, piece_rows)
    grads = lax.dot_general(
        cot_rows, o_weight, (((1,), (1,)), ((), ())), preferred_element_type=F32
    ).astype(BF16)
    returned = (
        swap(grads.reshape(tower_count, CAP, piece_rows))
        .reshape(NGROUP, group_size, CAP, piece_rows)
        .transpose(0, 2, 1, 3)
        .reshape(NGROUP * CAP, width)
    )
    attn_grad = lax.dot_general(
        one_hot, returned, (((0,), (0,)), ((), ())), preferred_element_type=F32
    ).astype(BF16)
    cot_parts = []
    for flip in range(dp_count):
        part = lax.dynamic_slice_in_dim(cot_rows, (dp_idx ^ flip) * piece_cols, piece_cols, 1)
        cot_parts.append(flip_over("dp", part, flip) if flip else part)
    attn_parts = gather_flips(attn_rows)
    return attn_grad, weight_grad_of([attn_parts[flip] for flip in range(dp_count)], cot_parts)


def per_device(*args):
    if lax.axis_size("tower") == NGROUP:
        return small_towers(*args)
    return large_towers(*args)


def solution(mesh):
    return jax.shard_map(
        per_device,
        mesh=mesh,
        in_specs=(
            P(("dp", "tower"), None),
            P(("dp", "tower"), None),
            P(("dp", "tower")),
            P(),
            P("tower", None),
        ),
        out_specs=(P(("dp", "tower"), None), P("tower", "dp")),
        check_vma=False,
    )
```

```python
import functools

import jax
import jax.numpy as jnp
from jax import lax
from jax.experimental import pallas as pl
from jax.experimental.pallas import tpu as pltpu
from jax.sharding import PartitionSpec as P


NGROUP = 8
KINDS = 3
CAP = 24
BF16 = jnp.bfloat16
F32 = jnp.float32
I32 = jnp.int32


MIB = 1 << 20


def grant(mib):
    return pltpu.CompilerParams(vmem_limit_bytes=mib * MIB)


def kept_in_hbm(value):
    return pltpu.with_memory_space_constraint(value, pltpu.HBM)


def cost(flops, moved):
    return pl.CostEstimate(flops=flops, bytes_accessed=moved, transcendentals=0)


RING = NGROUP // 2
STEPS = (0, 1, 3, 2)


def block_to(group, tower_idx):
    steps = (group // 2 - jnp.right_shift(tower_idx, 1)) & (RING - 1)
    place = jnp.int32(0)
    for at, step in enumerate(STEPS):
        place = jnp.where(steps == step, at, place)
    return place * 2 + ((group & 1) ^ (tower_idx & 1))


def target_of(tower_idx, block):
    return (tower_idx // 2 + STEPS[block // 2]) % RING * 2 + (tower_idx + block) % 2


def dispatch_matrix(tower_idx, kinds_ref, modal_row):
    tokens = modal_row.shape[1]
    earlier = lax.broadcasted_iota(I32, (tokens, tokens), 0) < lax.broadcasted_iota(
        I32, (tokens, tokens), 1
    )
    kind_rows = lax.broadcasted_iota(I32, (8, tokens), 0)
    member = jnp.where(kind_rows == modal_row, 1.0, 0.0)
    before = jnp.dot(
        member.astype(BF16),
        jnp.where(earlier, 1.0, 0.0).astype(BF16),
        preferred_element_type=F32,
    )
    order_in = jnp.sum(member * before, axis=0, keepdims=True)
    kinds = [kinds_ref[g] for g in range(NGROUP)]
    seen = [jnp.int32(0)] * KINDS
    ranks = []
    for g in range(NGROUP):
        rank = jnp.int32(0)
        for m in range(KINDS):
            hit = kinds[g] == m
            rank = jnp.where(hit, seen[m], rank)
            seen[m] = seen[m] + jnp.where(hit, 1, 0)
        ranks.append(rank)
    how_many = jnp.zeros((1, tokens), F32)
    for m in range(KINDS):
        how_many = jnp.where(modal_row == m, seen[m].astype(F32), how_many)
    inverse = 1.0 / jnp.maximum(how_many, 1.0)
    slot_idx = jnp.floor((order_in + 0.5) * inverse)
    shifted = order_in + tower_idx.astype(F32)
    target = shifted - how_many * jnp.floor((shifted + 0.5) * inverse)
    target = target.astype(I32)
    block = jnp.zeros((1, tokens), I32)
    for g in range(NGROUP):
        chosen = (modal_row == kinds[g]) & (target == ranks[g])
        block = jnp.where(chosen, block_to(g, tower_idx), block)
    place = block * CAP + slot_idx.astype(I32)
    slots = lax.broadcasted_iota(I32, (NGROUP * CAP, tokens), 0)
    return jnp.where(slots == place, 1.0, 0.0).astype(BF16)


def first_dispatch_kernel(
    chunks, blocks, tower_ref, kinds_hbm, modal_hbm, rows_hbm, one_hot_ref, *refs
):
    out_refs, (kinds_ref, modal_ref, rows_ref, known, arrived) = refs[:-5], refs[-5:]
    first, last = min(blocks) * CAP, (max(blocks) + 1) * CAP
    width = rows_ref.shape[1] // chunks
    tables = [
        pltpu.make_async_copy(kinds_hbm, kinds_ref, known.at[0]),
        pltpu.make_async_copy(modal_hbm, modal_ref, known.at[1]),
    ]
    for table in tables:
        table.start()
    copies = []
    for c in range(chunks):
        columns = pl.ds(c * width, width)
        copies.append(
            pltpu.make_async_copy(rows_hbm.at[:, columns], rows_ref.at[:, columns], arrived.at[c])
        )
        copies[c].start()
    for table in tables:
        table.wait()
    one_hot_ref[...] = dispatch_matrix(tower_ref[0], kinds_ref, modal_ref[...])
    for c in range(chunks):
        columns = pl.ds(c * width, width)
        copies[c].wait()
        placed = jnp.dot(
            one_hot_ref[first:last, :], rows_ref[:, columns], preferred_element_type=F32
        )
        for k, out_ref in zip(blocks, out_refs):
            at = k * CAP - first
            out_ref[:, columns] = placed[at : at + CAP, :].astype(BF16)


def dispatch_kernel(blocks, one_hot_ref, rows_ref, *out_refs):
    placed = jnp.dot(one_hot_ref[...], rows_ref[...], preferred_element_type=F32)
    for k, out_ref in zip(blocks, out_refs):
        out_ref[...] = placed[k * CAP : (k + 1) * CAP, :].astype(BF16)


def dispatch_first(tower_idx, kinds, modal_row, rows, blocks):
    tokens, width = rows.shape
    chunks = 4
    slots = NGROUP * CAP
    in_smem = pl.BlockSpec(memory_space=pltpu.SMEM)
    in_vmem = pl.BlockSpec(memory_space=pltpu.VMEM)
    out = pl.pallas_call(
        functools.partial(first_dispatch_kernel, chunks, blocks),
        in_specs=[in_smem] + [pl.BlockSpec(memory_space=pltpu.HBM)] * 3,
        out_specs=[in_vmem] * (len(blocks) + 1),
        out_shape=[jax.ShapeDtypeStruct((slots, tokens), BF16)]
        + [jax.ShapeDtypeStruct((CAP, width), BF16)] * len(blocks),
        scratch_shapes=[
            pltpu.SMEM((NGROUP,), I32),
            pltpu.VMEM((1, tokens), I32),
            pltpu.VMEM((tokens, width), BF16),
            pltpu.SemaphoreType.DMA((2,)),
            pltpu.SemaphoreType.DMA((chunks,)),
        ],
        cost_estimate=cost(2 * slots * tokens * width, 2 * (tokens + slots) * width),
        compiler_params=grant(12),
        name="dispatch_cot",
    )(tower_idx, *map(kept_in_hbm, (kinds, modal_row, rows)))
    return out[0], dict(zip(blocks, out[1:]))


def dispatch_next(one_hot, rows, blocks, mib):
    tokens, width = rows.shape
    block = min(1024, width)
    slots = one_hot.shape[0]
    out = pl.pallas_call(
        functools.partial(dispatch_kernel, blocks),
        grid=(width // block,),
        in_specs=[
            pl.BlockSpec((slots, tokens), lambda i: (0, 0)),
            pl.BlockSpec((tokens, block), lambda i: (0, i)),
        ],
        out_specs=[pl.BlockSpec((CAP, block), lambda i: (0, i))] * len(blocks),
        out_shape=[jax.ShapeDtypeStruct((CAP, width), BF16)] * len(blocks),
        cost_estimate=cost(2 * slots * tokens * width, 2 * (tokens + slots) * width),
        compiler_params=grant(mib),
    )(one_hot, kept_in_hbm(rows))
    return dict(zip(blocks, out))


def pieces_kernel(count, dp_ref, *refs):
    block_refs, out_refs = refs[:count], refs[count:]
    columns = out_refs[0].shape[1]
    for f, out_ref in enumerate(out_refs):
        first = pl.multiple_of(jnp.bitwise_xor(dp_ref[0], jnp.int32(f)) * columns, 128)
        for k, block_ref in enumerate(block_refs):
            out_ref[k * CAP : (k + 1) * CAP, :] = block_ref[:, pl.ds(first, columns)]


def column_pieces(dp_idx, blocks):
    pieces = lax.axis_size("dp")
    width = blocks[0].shape[1]
    rows = len(blocks) * CAP
    whole = pl.BlockSpec(memory_space=pltpu.VMEM)
    return pl.pallas_call(
        functools.partial(pieces_kernel, len(blocks)),
        in_specs=[pl.BlockSpec(memory_space=pltpu.SMEM)] + [whole] * len(blocks),
        out_specs=[whole] * pieces,
        out_shape=[jax.ShapeDtypeStruct((rows, width // pieces), BF16)] * pieces,
        cost_estimate=cost(0, 4 * rows * width),
        compiler_params=grant(8),
        name="column_pieces",
    )(dp_idx, *blocks)


def token_grad_kernel(pieces, parts, dp_ref, *refs):
    cot_refs, weight_refs = refs[: pieces * parts], refs[pieces * parts : pieces * (parts + 1)]
    out_refs, rows_refs = refs[pieces * (parts + 1) : -pieces], refs[-pieces:]

    @pl.when(pl.program_id(0) == 0)
    def _():
        for f, rows_ref in enumerate(rows_refs):
            at = 0
            for cot_ref in cot_refs[f::pieces]:
                rows_ref[at : at + cot_ref.shape[0], :] = cot_ref[...]
                at += cot_ref.shape[0]

    grads = None
    for rows_ref, weight_ref in zip(rows_refs, weight_refs):
        term = lax.dot_general(
            rows_ref[...], weight_ref[...], (((1,), (1,)), ((), ())), preferred_element_type=F32
        )
        grads = term if grads is None else grads + term
    for k, out_ref in enumerate(out_refs):
        out_ref[...] = grads[k * CAP : (k + 1) * CAP, :].astype(BF16)


def token_grad(dp_idx, cot_pieces, weight):
    features, width = weight.shape
    pieces = len(cot_pieces[0])
    columns = width // pieces
    slots = NGROUP * CAP
    block = min(512, features)

    def weight_spec(f):
        return pl.BlockSpec((block, columns), lambda i, dp_ref: (i, jnp.bitwise_xor(dp_ref[0], f)))

    flat = [piece for part in cot_pieces for piece in part]
    return list(
        pl.pallas_call(
            functools.partial(token_grad_kernel, pieces, len(cot_pieces)),
            grid_spec=pltpu.PrefetchScalarGridSpec(
                num_scalar_prefetch=1,
                grid=(features // block,),
                in_specs=[pl.BlockSpec(piece.shape, lambda i, dp_ref: (0, 0)) for piece in flat]
                + [weight_spec(f) for f in range(pieces)],
                out_specs=[pl.BlockSpec((CAP, block), lambda i, dp_ref: (0, i))] * NGROUP,
                scratch_shapes=[pltpu.VMEM((slots, columns), BF16)] * pieces,
            ),
            out_shape=[jax.ShapeDtypeStruct((CAP, features), BF16)] * NGROUP,
            cost_estimate=cost(
                2 * slots * features * width, 2 * (features * width + 2 * slots * width)
            ),
            compiler_params=grant(24),
            name="token_grad",
        )(dp_idx, *flat, *[weight] * pieces)
    )


def rows_back(one_hot_ref, first, got_refs, rows_ref, columns):
    for k, got_ref in enumerate(got_refs):
        rows_ref[k * CAP : (k + 1) * CAP, columns] = got_ref[:, columns]
    return lax.dot_general(
        one_hot_ref[first * CAP : (first + len(got_refs)) * CAP, :],
        rows_ref[:, columns],
        (((0,), (0,)), ((), ())),
        preferred_element_type=F32,
    )


def combine_first_kernel(chunks, one_hot_ref, *refs):
    got_refs, out_ref, rows_ref = refs[:-2], refs[-2], refs[-1]
    width = out_ref.shape[1] // chunks
    for c in range(chunks):
        columns = pl.ds(c * width, width)
        out_ref[:, columns] = rows_back(one_hot_ref, 0, got_refs, rows_ref, columns).astype(BF16)


def combine_last_kernel(chunks, first, one_hot_ref, partial_ref, *refs):
    got_refs, out_hbm, rows_ref, out_ref, written = refs[:-4], *refs[-4:]
    width = out_ref.shape[1] // chunks
    copies = []
    for c in range(chunks):
        columns = pl.ds(c * width, width)
        total = rows_back(one_hot_ref, first, got_refs, rows_ref, columns)
        out_ref[:, columns] = (total + partial_ref[:, columns].astype(F32)).astype(BF16)
        copies.append(
            pltpu.make_async_copy(out_ref.at[:, columns], out_hbm.at[:, columns], written.at[c])
        )
        copies[c].start()
    for copy in copies:
        copy.wait()


def combine_first(one_hot, blocks):
    tokens = one_hot.shape[1]
    width = blocks[0].shape[1]
    rows = len(blocks) * CAP
    whole = pl.BlockSpec(memory_space=pltpu.VMEM)
    return pl.pallas_call(
        functools.partial(combine_first_kernel, 4),
        in_specs=[whole] * (1 + len(blocks)),
        out_specs=whole,
        out_shape=jax.ShapeDtypeStruct((tokens, width), BF16),
        scratch_shapes=[pltpu.VMEM((rows, width), BF16)],
        cost_estimate=cost(2 * rows * tokens * width, 2 * (tokens + rows) * width),
        compiler_params=grant(12),
        name="combine_first",
    )(one_hot, *blocks)


def combine_last(one_hot, partial, blocks):
    tokens, width = partial.shape
    chunks = 4
    rows = len(blocks) * CAP
    whole = pl.BlockSpec(memory_space=pltpu.VMEM)
    return pl.pallas_call(
        functools.partial(combine_last_kernel, chunks, NGROUP - len(blocks)),
        in_specs=[whole] * (2 + len(blocks)),
        out_specs=pl.BlockSpec(memory_space=pl.ANY),
        out_shape=jax.ShapeDtypeStruct((tokens, width), BF16),
        scratch_shapes=[
            pltpu.VMEM((rows, width), BF16),
            pltpu.VMEM((tokens, width), BF16),
            pltpu.SemaphoreType.DMA((chunks,)),
        ],
        cost_estimate=cost(2 * rows * tokens * width, 2 * (2 * tokens + rows) * width),
        compiler_params=grant(12),
        name="combine_last",
    )(one_hot, partial, *blocks)


def join_kernel(*refs):
    at = 0
    for ref in refs[:-1]:
        rows = ref.shape[0]
        refs[-1][at : at + rows, :] = ref[...]
        at += rows


def join_rows(blocks):
    if len(blocks) == 1:
        return blocks[0]
    rows = sum(block.shape[0] for block in blocks)
    width = blocks[0].shape[1]
    whole = pl.BlockSpec(memory_space=pltpu.VMEM)
    return pl.pallas_call(
        join_kernel,
        in_specs=[whole] * len(blocks),
        out_specs=whole,
        out_shape=jax.ShapeDtypeStruct((rows, width), BF16),
        cost_estimate=cost(0, 4 * rows * width),
        compiler_params=grant(8),
        name="join_rows",
    )(*blocks)


def weight_grad_kernel(n_attn, n_cot, *refs):
    attn_refs, cot_refs = refs[:n_attn], refs[n_attn : n_attn + n_cot]
    out_ref, attn_rows_ref, cot_rows_ref = refs[n_attn + n_cot :]

    @pl.when(pl.program_id(0) == 0)
    def _():
        at = 0
        for cot_ref in cot_refs:
            rows = cot_ref.shape[0]
            cot_rows_ref[at : at + rows, :] = cot_ref[...]
            at += rows

    at = 0
    for attn_ref in attn_refs:
        rows = attn_ref.shape[0]
        attn_rows_ref[at : at + rows, :] = attn_ref[...]
        at += rows
    out_ref[...] = lax.dot_general(
        attn_rows_ref[...],
        cot_rows_ref[...],
        (((0,), (0,)), ((), ())),
        preferred_element_type=F32,
    ).astype(out_ref.dtype)


def weight_grad_of(attn_parts, cot_parts):
    features = attn_parts[0].shape[1]
    columns = cot_parts[0].shape[1]
    rows = sum(part.shape[0] for part in attn_parts)
    block = min(512, features)
    return pl.pallas_call(
        functools.partial(weight_grad_kernel, len(attn_parts), len(cot_parts)),
        grid=(features // block,),
        in_specs=[pl.BlockSpec((part.shape[0], block), lambda i: (0, i)) for part in attn_parts]
        + [pl.BlockSpec((part.shape[0], columns), lambda i: (0, 0)) for part in cot_parts],
        out_specs=pl.BlockSpec((block, columns), lambda i: (i, 0)),
        out_shape=jax.ShapeDtypeStruct((features, columns), BF16),
        scratch_shapes=[pltpu.VMEM((rows, block), BF16), pltpu.VMEM((rows, columns), BF16)],
        cost_estimate=cost(
            2 * rows * features * columns, 2 * (rows * (features + columns) + features * columns)
        ),
        compiler_params=grant(20),
        name="weight_grad",
    )(*attn_parts, *cot_parts)


def flip_over(axis, value, flip):
    size = lax.axis_size(axis)
    return lax.ppermute(value, axis, [(i, i ^ flip) for i in range(size)])


def swap_blocks(blocks, back=False):
    got = [blocks[0]]
    for k in range(1, NGROUP):
        pairs = [(t, target_of(t, k)) for t in range(NGROUP)]
        if back:
            pairs = [(target, source) for source, target in pairs]
        got.append(lax.ppermute(blocks[k], "tower", pairs))
    return got


def gather_flips(value):
    parts = {0: value}
    flip = lax.axis_size("dp") // 2
    while flip:
        for known in list(parts):
            parts[known ^ flip] = flip_over("dp", parts[known], flip)
        flip //= 2
    return parts


COT_PARTS = {"cot_early": (0, 1, 2, 3), "cot_late": (4, 5, 6, 7)}
ATTN_PARTS = {"attn_a": (0, 1), "attn_b": (2,), "attn_c": (3, 4, 5), "attn_d": (6, 7)}
LAST = (6, 7)
FIRST = (2, 3)


def small_towers(attn_out, out_cot, modality, group_modality, o_weight):
    tower_idx = lax.axis_index("tower").astype(I32)
    dp_idx = lax.axis_index("dp").astype(I32).reshape(1)
    dp_count = lax.axis_size("dp")

    every = tuple(range(NGROUP))
    rest = tuple(k for k in every if k not in FIRST)
    one_hot, cot_blocks = dispatch_first(
        tower_idx.reshape(1), group_modality, modality.reshape(1, -1), out_cot, FIRST
    )
    cot_blocks |= dispatch_next(one_hot, out_cot, rest, 12)
    attn_blocks = dispatch_next(one_hot, attn_out, every, 56)
    cot_got = swap_blocks(cot_blocks)
    attn_got = swap_blocks(attn_blocks)
    cot_pieces, cot_moved = [], []
    for blocks in COT_PARTS.values():
        pieces = column_pieces(dp_idx, [cot_got[k] for k in blocks])
        cot_pieces.append(pieces)
        cot_moved.append(
            [flip_over("dp", piece, flip) if flip else piece for flip, piece in enumerate(pieces)]
        )
    cot_parts = [moved[flip] for flip in range(dp_count) for moved in cot_moved]
    grads = token_grad(dp_idx, cot_pieces, o_weight)
    returned = swap_blocks(grads, back=True)
    partial = combine_first(one_hot, [returned[k] for k in range(NGROUP) if k not in LAST])
    attn_grad = combine_last(one_hot, partial, [returned[k] for k in LAST])

    parts = []
    for blocks in ATTN_PARTS.values():
        joined = join_rows([attn_got[k] for k in blocks])
        parts.append(gather_flips(joined))
    attn_parts = [part[flip] for flip in range(dp_count) for part in parts]
    return attn_grad, weight_grad_of(attn_parts, cot_parts)


def large_towers(attn_out, out_cot, modality, group_modality, o_weight):
    tower_idx = lax.axis_index("tower").astype(I32)
    tower_count = lax.axis_size("tower")
    dp_idx = lax.axis_index("dp")
    dp_count = lax.axis_size("dp")
    group_size = tower_count // NGROUP
    piece_rows, width = o_weight.shape
    tokens = attn_out.shape[0]
    piece_cols = width // dp_count
    modal_row = modality.reshape(1, tokens)
    group_ids = jnp.arange(NGROUP, dtype=I32)
    member = modal_row == jnp.arange(KINDS, dtype=I32)[:, None]
    before = jnp.cumsum(member.astype(I32), axis=1) - 1
    order_in = jnp.sum(jnp.where(member, before, 0), axis=0)
    group_of = (group_modality[:, None] == jnp.arange(KINDS, dtype=I32)[None, :]).astype(I32)
    group_rank = jnp.sum((jnp.cumsum(group_of, axis=0) - group_of) * group_of, axis=1)
    how_many = jnp.sum(member * jnp.sum(group_of, axis=0)[:, None], axis=0)
    target = (order_in + tower_idx) % how_many
    chosen = (group_modality[:, None] == modal_row) & (group_rank[:, None] == target[None, :])
    routed = jnp.sum(chosen.astype(I32) * group_ids[:, None], axis=0)
    place = routed * CAP + order_in // how_many
    one_hot = (place[None, :] == jnp.arange(NGROUP * CAP, dtype=I32)[:, None]).astype(BF16)

    def swap(value):
        return lax.all_to_all(value, "tower", split_axis=0, concat_axis=0, tiled=True)

    cot_group = jnp.dot(one_hot, out_cot, preferred_element_type=F32).astype(BF16)
    attn_group = jnp.dot(one_hot, attn_out, preferred_element_type=F32).astype(BF16)
    cot_send = jnp.broadcast_to(
        cot_group.reshape(NGROUP, 1, CAP, width), (NGROUP, group_size, CAP, width)
    ).reshape(tower_count, CAP, width)
    attn_send = (
        attn_group.reshape(NGROUP, CAP, group_size, piece_rows)
        .transpose(0, 2, 1, 3)
        .reshape(tower_count, CAP, piece_rows)
    )
    cot_rows = swap(cot_send).reshape(tower_count * CAP, width)
    attn_rows = swap(attn_send).reshape(tower_count * CAP, piece_rows)
    grads = lax.dot_general(
        cot_rows, o_weight, (((1,), (1,)), ((), ())), preferred_element_type=F32
    ).astype(BF16)
    returned = (
        swap(grads.reshape(tower_count, CAP, piece_rows))
        .reshape(NGROUP, group_size, CAP, piece_rows)
        .transpose(0, 2, 1, 3)
        .reshape(NGROUP * CAP, width)
    )
    attn_grad = lax.dot_general(
        one_hot, returned, (((0,), (0,)), ((), ())), preferred_element_type=F32
    ).astype(BF16)
    cot_parts = []
    for flip in range(dp_count):
        part = lax.dynamic_slice_in_dim(cot_rows, (dp_idx ^ flip) * piece_cols, piece_cols, 1)
        cot_parts.append(flip_over("dp", part, flip) if flip else part)
    attn_parts = gather_flips(attn_rows)
    return attn_grad, weight_grad_of([attn_parts[flip] for flip in range(dp_count)], cot_parts)


def per_device(*args):
    if lax.axis_size("tower") == NGROUP:
        return small_towers(*args)
    return large_towers(*args)


def solution(mesh):
    return jax.shard_map(
        per_device,
        mesh=mesh,
        in_specs=(
            P(("dp", "tower"), None),
            P(("dp", "tower"), None),
            P(("dp", "tower")),
            P(),
            P("tower", None),
        ),
        out_specs=(P(("dp", "tower"), None), P("tower", "dp")),
        check_vma=False,
    )
```

```python
import functools

import jax
import jax.numpy as jnp
from jax import lax
from jax.experimental import pallas as pl
from jax.experimental.pallas import tpu as pltpu
from jax.sharding import PartitionSpec as P


NGROUP = 8
KINDS = 3
CAP = 24
TOWER, DP = "tower", "dp"
BF16 = jnp.bfloat16
F32 = jnp.float32
I32 = jnp.int32


MIB = 1 << 20


def grant(mib):
    return pltpu.CompilerParams(vmem_limit_bytes=mib * MIB)


def kept_in_hbm(value):
    return pltpu.with_memory_space_constraint(value, pltpu.HBM)


def cost(flops, moved):
    return pl.CostEstimate(flops=flops, bytes_accessed=moved, transcendentals=0)


RING = NGROUP // 2
STEPS = (0, 1, 3, 2)


def block_to(group, tower_idx):
    steps = (group // 2 - jnp.right_shift(tower_idx, 1)) & (RING - 1)
    place = jnp.int32(0)
    for at, step in enumerate(STEPS):
        place = jnp.where(steps == step, at, place)
    return place * 2 + ((group & 1) ^ (tower_idx & 1))


def target_of(tower_idx, block):
    return (tower_idx // 2 + STEPS[block // 2]) % RING * 2 + (tower_idx + block) % 2


def dispatch_matrix(tower_idx, kinds_ref, modal_row):
    tokens = modal_row.shape[1]
    earlier = lax.broadcasted_iota(I32, (tokens, tokens), 0) < lax.broadcasted_iota(
        I32, (tokens, tokens), 1
    )
    kind_rows = lax.broadcasted_iota(I32, (8, tokens), 0)
    member = jnp.where(kind_rows == modal_row, 1.0, 0.0)
    before = jnp.dot(
        member.astype(BF16),
        jnp.where(earlier, 1.0, 0.0).astype(BF16),
        preferred_element_type=F32,
    )
    order_in = jnp.sum(member * before, axis=0, keepdims=True)
    kinds = [kinds_ref[g] for g in range(NGROUP)]
    seen = [jnp.int32(0)] * KINDS
    ranks = []
    for g in range(NGROUP):
        rank = jnp.int32(0)
        for m in range(KINDS):
            hit = kinds[g] == m
            rank = jnp.where(hit, seen[m], rank)
            seen[m] = seen[m] + jnp.where(hit, 1, 0)
        ranks.append(rank)
    how_many = jnp.zeros((1, tokens), F32)
    for m in range(KINDS):
        how_many = jnp.where(modal_row == m, seen[m].astype(F32), how_many)
    inverse = 1.0 / jnp.maximum(how_many, 1.0)
    slot_idx = jnp.floor((order_in + 0.5) * inverse)
    shifted = order_in + tower_idx.astype(F32)
    target = shifted - how_many * jnp.floor((shifted + 0.5) * inverse)
    target = target.astype(I32)
    block = jnp.zeros((1, tokens), I32)
    for g in range(NGROUP):
        chosen = (modal_row == kinds[g]) & (target == ranks[g])
        block = jnp.where(chosen, block_to(g, tower_idx), block)
    place = block * CAP + slot_idx.astype(I32)
    slots = lax.broadcasted_iota(I32, (NGROUP * CAP, tokens), 0)
    return jnp.where(slots == place, 1.0, 0.0).astype(BF16)


def first_dispatch_kernel(
    chunks, blocks, tower_ref, kinds_hbm, modal_hbm, rows_hbm, one_hot_ref, *refs
):
    out_refs, (kinds_ref, modal_ref, rows_ref, known, arrived) = refs[:-5], refs[-5:]
    first, last = min(blocks) * CAP, (max(blocks) + 1) * CAP
    width = rows_ref.shape[1] // chunks
    tables = [
        pltpu.make_async_copy(kinds_hbm, kinds_ref, known.at[0]),
        pltpu.make_async_copy(modal_hbm, modal_ref, known.at[1]),
    ]
    for table in tables:
        table.start()
    copies = []
    for c in range(chunks):
        columns = pl.ds(c * width, width)
        copies.append(
            pltpu.make_async_copy(rows_hbm.at[:, columns], rows_ref.at[:, columns], arrived.at[c])
        )
        copies[c].start()
    for table in tables:
        table.wait()
    one_hot_ref[...] = dispatch_matrix(tower_ref[0], kinds_ref, modal_ref[...])
    for c in range(chunks):
        columns = pl.ds(c * width, width)
        copies[c].wait()
        placed = jnp.dot(
            one_hot_ref[first:last, :], rows_ref[:, columns], preferred_element_type=F32
        )
        for k, out_ref in zip(blocks, out_refs):
            at = k * CAP - first
            out_ref[:, columns] = placed[at : at + CAP, :].astype(BF16)


def dispatch_kernel(blocks, one_hot_ref, rows_ref, *out_refs):
    placed = jnp.dot(one_hot_ref[...], rows_ref[...], preferred_element_type=F32)
    for k, out_ref in zip(blocks, out_refs):
        out_ref[...] = placed[k * CAP : (k + 1) * CAP, :].astype(BF16)


def dispatch_first(tower_idx, kinds, modal_row, rows, blocks):
    tokens, width = rows.shape
    chunks = 4
    slots = NGROUP * CAP
    in_smem = pl.BlockSpec(memory_space=pltpu.SMEM)
    in_vmem = pl.BlockSpec(memory_space=pltpu.VMEM)
    out = pl.pallas_call(
        functools.partial(first_dispatch_kernel, chunks, blocks),
        in_specs=[in_smem] + [pl.BlockSpec(memory_space=pltpu.HBM)] * 3,
        out_specs=[in_vmem] * (len(blocks) + 1),
        out_shape=[jax.ShapeDtypeStruct((slots, tokens), BF16)]
        + [jax.ShapeDtypeStruct((CAP, width), BF16)] * len(blocks),
        scratch_shapes=[
            pltpu.SMEM((NGROUP,), I32),
            pltpu.VMEM((1, tokens), I32),
            pltpu.VMEM((tokens, width), BF16),
            pltpu.SemaphoreType.DMA((2,)),
            pltpu.SemaphoreType.DMA((chunks,)),
        ],
        cost_estimate=cost(2 * slots * tokens * width, 2 * (tokens + slots) * width),
        compiler_params=grant(12),
        name="dispatch_cot",
    )(tower_idx, *map(kept_in_hbm, (kinds, modal_row, rows)))
    return out[0], dict(zip(blocks, out[1:]))


def dispatch_next(one_hot, rows, blocks, mib):
    tokens, width = rows.shape
    block = min(1024, width)
    slots = one_hot.shape[0]
    out = pl.pallas_call(
        functools.partial(dispatch_kernel, blocks),
        grid=(width // block,),
        in_specs=[
            pl.BlockSpec((slots, tokens), lambda i: (0, 0)),
            pl.BlockSpec((tokens, block), lambda i: (0, i)),
        ],
        out_specs=[pl.BlockSpec((CAP, block), lambda i: (0, i))] * len(blocks),
        out_shape=[jax.ShapeDtypeStruct((CAP, width), BF16)] * len(blocks),
        cost_estimate=cost(2 * slots * tokens * width, 2 * (tokens + slots) * width),
        compiler_params=grant(mib),
    )(one_hot, kept_in_hbm(rows))
    return dict(zip(blocks, out))


def pieces_kernel(count, dp_ref, *refs):
    block_refs, out_refs = refs[:count], refs[count:]
    columns = out_refs[0].shape[1]
    for f, out_ref in enumerate(out_refs):
        first = pl.multiple_of(jnp.bitwise_xor(dp_ref[0], jnp.int32(f)) * columns, 128)
        for k, block_ref in enumerate(block_refs):
            out_ref[k * CAP : (k + 1) * CAP, :] = block_ref[:, pl.ds(first, columns)]


def column_pieces(dp_idx, blocks):
    pieces = lax.axis_size(DP)
    width = blocks[0].shape[1]
    rows = len(blocks) * CAP
    whole = pl.BlockSpec(memory_space=pltpu.VMEM)
    return pl.pallas_call(
        functools.partial(pieces_kernel, len(blocks)),
        in_specs=[pl.BlockSpec(memory_space=pltpu.SMEM)] + [whole] * len(blocks),
        out_specs=[whole] * pieces,
        out_shape=[jax.ShapeDtypeStruct((rows, width // pieces), BF16)] * pieces,
        cost_estimate=cost(0, 4 * rows * width),
        compiler_params=grant(8),
        name="column_pieces",
    )(dp_idx, *blocks)


def token_grad_kernel(pieces, parts, dp_ref, *refs):
    cot_refs, weight_refs = refs[: pieces * parts], refs[pieces * parts : pieces * (parts + 1)]
    out_refs, rows_refs = refs[pieces * (parts + 1) : -pieces], refs[-pieces:]

    @pl.when(pl.program_id(0) == 0)
    def _():
        for f, rows_ref in enumerate(rows_refs):
            at = 0
            for cot_ref in cot_refs[f::pieces]:
                rows_ref[at : at + cot_ref.shape[0], :] = cot_ref[...]
                at += cot_ref.shape[0]

    grads = None
    for rows_ref, weight_ref in zip(rows_refs, weight_refs):
        term = lax.dot_general(
            rows_ref[...], weight_ref[...], (((1,), (1,)), ((), ())), preferred_element_type=F32
        )
        grads = term if grads is None else grads + term
    for k, out_ref in enumerate(out_refs):
        out_ref[...] = grads[k * CAP : (k + 1) * CAP, :].astype(BF16)


def token_grad(dp_idx, cot_pieces, weight):
    features, width = weight.shape
    pieces = len(cot_pieces[0])
    columns = width // pieces
    slots = NGROUP * CAP
    block = min(512, features)

    def weight_spec(f):
        return pl.BlockSpec((block, columns), lambda i, dp_ref: (i, jnp.bitwise_xor(dp_ref[0], f)))

    flat = [piece for part in cot_pieces for piece in part]
    return list(
        pl.pallas_call(
            functools.partial(token_grad_kernel, pieces, len(cot_pieces)),
            grid_spec=pltpu.PrefetchScalarGridSpec(
                num_scalar_prefetch=1,
                grid=(features // block,),
                in_specs=[pl.BlockSpec(piece.shape, lambda i, dp_ref: (0, 0)) for piece in flat]
                + [weight_spec(f) for f in range(pieces)],
                out_specs=[pl.BlockSpec((CAP, block), lambda i, dp_ref: (0, i))] * NGROUP,
                scratch_shapes=[pltpu.VMEM((slots, columns), BF16)] * pieces,
            ),
            out_shape=[jax.ShapeDtypeStruct((CAP, features), BF16)] * NGROUP,
            cost_estimate=cost(
                2 * slots * features * width, 2 * (features * width + 2 * slots * width)
            ),
            compiler_params=grant(24),
        )(dp_idx, *flat, *[weight] * pieces)
    )


def rows_back(one_hot_ref, first, got_refs, rows_ref, columns):
    for k, got_ref in enumerate(got_refs):
        rows_ref[k * CAP : (k + 1) * CAP, columns] = got_ref[:, columns]
    return lax.dot_general(
        one_hot_ref[first * CAP : (first + len(got_refs)) * CAP, :],
        rows_ref[:, columns],
        (((0,), (0,)), ((), ())),
        preferred_element_type=F32,
    )


def combine_first_kernel(chunks, one_hot_ref, *refs):
    got_refs, out_ref, rows_ref = refs[:-2], refs[-2], refs[-1]
    width = out_ref.shape[1] // chunks
    for c in range(chunks):
        columns = pl.ds(c * width, width)
        out_ref[:, columns] = rows_back(one_hot_ref, 0, got_refs, rows_ref, columns).astype(BF16)


def combine_last_kernel(chunks, first, one_hot_ref, partial_ref, *refs):
    got_refs, out_hbm, rows_ref, out_ref, written = refs[:-4], *refs[-4:]
    width = out_ref.shape[1] // chunks
    copies = []
    for c in range(chunks):
        columns = pl.ds(c * width, width)
        total = rows_back(one_hot_ref, first, got_refs, rows_ref, columns)
        out_ref[:, columns] = (total + partial_ref[:, columns].astype(F32)).astype(BF16)
        copies.append(
            pltpu.make_async_copy(out_ref.at[:, columns], out_hbm.at[:, columns], written.at[c])
        )
        copies[c].start()
    for copy in copies:
        copy.wait()


def combine_first(one_hot, blocks):
    tokens = one_hot.shape[1]
    width = blocks[0].shape[1]
    rows = len(blocks) * CAP
    whole = pl.BlockSpec(memory_space=pltpu.VMEM)
    return pl.pallas_call(
        functools.partial(combine_first_kernel, 4),
        in_specs=[whole] * (1 + len(blocks)),
        out_specs=whole,
        out_shape=jax.ShapeDtypeStruct((tokens, width), BF16),
        scratch_shapes=[pltpu.VMEM((rows, width), BF16)],
        cost_estimate=cost(2 * rows * tokens * width, 2 * (tokens + rows) * width),
        compiler_params=grant(12),
    )(one_hot, *blocks)


def combine_last(one_hot, partial, blocks):
    tokens, width = partial.shape
    chunks = 4
    rows = len(blocks) * CAP
    whole = pl.BlockSpec(memory_space=pltpu.VMEM)
    return pl.pallas_call(
        functools.partial(combine_last_kernel, chunks, NGROUP - len(blocks)),
        in_specs=[whole] * (2 + len(blocks)),
        out_specs=pl.BlockSpec(memory_space=pl.ANY),
        out_shape=jax.ShapeDtypeStruct((tokens, width), BF16),
        scratch_shapes=[
            pltpu.VMEM((rows, width), BF16),
            pltpu.VMEM((tokens, width), BF16),
            pltpu.SemaphoreType.DMA((chunks,)),
        ],
        cost_estimate=cost(2 * rows * tokens * width, 2 * (2 * tokens + rows) * width),
        compiler_params=grant(12),
        name="combine_last",
    )(one_hot, partial, *blocks)


def join_kernel(*refs):
    at = 0
    for ref in refs[:-1]:
        rows = ref.shape[0]
        refs[-1][at : at + rows, :] = ref[...]
        at += rows


def join_rows(blocks):
    if len(blocks) == 1:
        return blocks[0]
    rows = sum(block.shape[0] for block in blocks)
    width = blocks[0].shape[1]
    whole = pl.BlockSpec(memory_space=pltpu.VMEM)
    return pl.pallas_call(
        join_kernel,
        in_specs=[whole] * len(blocks),
        out_specs=whole,
        out_shape=jax.ShapeDtypeStruct((rows, width), BF16),
        cost_estimate=cost(0, 4 * rows * width),
        compiler_params=grant(8),
        name="join_rows",
    )(*blocks)


def weight_grad_kernel(n_attn, n_cot, *refs):
    attn_refs, cot_refs = refs[:n_attn], refs[n_attn : n_attn + n_cot]
    out_ref, attn_rows_ref, cot_rows_ref = refs[n_attn + n_cot :]

    @pl.when(pl.program_id(0) == 0)
    def _():
        at = 0
        for cot_ref in cot_refs:
            rows = cot_ref.shape[0]
            cot_rows_ref[at : at + rows, :] = cot_ref[...]
            at += rows

    at = 0
    for attn_ref in attn_refs:
        rows = attn_ref.shape[0]
        attn_rows_ref[at : at + rows, :] = attn_ref[...]
        at += rows
    out_ref[...] = lax.dot_general(
        attn_rows_ref[...],
        cot_rows_ref[...],
        (((0,), (0,)), ((), ())),
        preferred_element_type=F32,
    ).astype(out_ref.dtype)


def weight_grad_of(attn_parts, cot_parts):
    features = attn_parts[0].shape[1]
    columns = cot_parts[0].shape[1]
    rows = sum(part.shape[0] for part in attn_parts)
    block = min(512, features)
    return pl.pallas_call(
        functools.partial(weight_grad_kernel, len(attn_parts), len(cot_parts)),
        grid=(features // block,),
        in_specs=[pl.BlockSpec((part.shape[0], block), lambda i: (0, i)) for part in attn_parts]
        + [pl.BlockSpec((part.shape[0], columns), lambda i: (0, 0)) for part in cot_parts],
        out_specs=pl.BlockSpec((block, columns), lambda i: (i, 0)),
        out_shape=jax.ShapeDtypeStruct((features, columns), BF16),
        scratch_shapes=[pltpu.VMEM((rows, block), BF16), pltpu.VMEM((rows, columns), BF16)],
        cost_estimate=cost(
            2 * rows * features * columns, 2 * (rows * (features + columns) + features * columns)
        ),
        compiler_params=grant(20),
    )(*attn_parts, *cot_parts)


def flip_over(axis, value, flip):
    size = lax.axis_size(axis)
    return lax.ppermute(value, axis, [(i, i ^ flip) for i in range(size)])


def swap_blocks(blocks, back=False):
    got = [blocks[0]]
    for k in range(1, NGROUP):
        pairs = [(t, target_of(t, k)) for t in range(NGROUP)]
        if back:
            pairs = [(target, source) for source, target in pairs]
        got.append(lax.ppermute(blocks[k], TOWER, pairs))
    return got


def gather_flips(value):
    parts = {0: value}
    flip = lax.axis_size(DP) // 2
    while flip:
        for known in list(parts):
            parts[known ^ flip] = flip_over(DP, parts[known], flip)
        flip //= 2
    return parts


COT_PARTS = {"ce": (0, 1, 2, 3), "cl": (4, 5, 6, 7)}
ATTN_PARTS = {"aa": (0, 1), "ab": (2,), "ac": (3, 4, 5), "ad": (6, 7)}
LAST = (6, 7)
FIRST = (2,)


def small_towers(attn_out, out_cot, modality, group_modality, o_weight):
    tower_idx = lax.axis_index(TOWER).astype(I32)
    dp_idx = lax.axis_index(DP).astype(I32).reshape(1)
    dp_count = lax.axis_size(DP)

    every = tuple(range(NGROUP))
    rest = tuple(k for k in every if k not in FIRST)
    one_hot, cot_blocks = dispatch_first(
        tower_idx.reshape(1), group_modality, modality.reshape(1, -1), out_cot, FIRST
    )
    cot_blocks |= dispatch_next(one_hot, out_cot, rest, 12)
    attn_blocks = dispatch_next(one_hot, attn_out, every, 56)
    cot_got = swap_blocks(cot_blocks)
    attn_got = swap_blocks(attn_blocks)
    cot_pieces, cot_moved = [], []
    for blocks in COT_PARTS.values():
        pieces = column_pieces(dp_idx, [cot_got[k] for k in blocks])
        cot_pieces.append(pieces)
        cot_moved.append(
            [flip_over(DP, piece, flip) if flip else piece for flip, piece in enumerate(pieces)]
        )
    cot_parts = [moved[flip] for flip in range(dp_count) for moved in cot_moved]
    grads = token_grad(dp_idx, cot_pieces, o_weight)
    returned = swap_blocks(grads, back=True)
    partial = combine_first(one_hot, [returned[k] for k in range(NGROUP) if k not in LAST])
    attn_grad = combine_last(one_hot, partial, [returned[k] for k in LAST])

    parts = []
    for blocks in ATTN_PARTS.values():
        joined = join_rows([attn_got[k] for k in blocks])
        parts.append(gather_flips(joined))
    attn_parts = [part[flip] for flip in range(dp_count) for part in parts]
    return attn_grad, weight_grad_of(attn_parts, cot_parts)


def large_towers(attn_out, out_cot, modality, group_modality, o_weight):
    tower_idx = lax.axis_index(TOWER).astype(I32)
    tower_count = lax.axis_size(TOWER)
    dp_idx = lax.axis_index(DP)
    dp_count = lax.axis_size(DP)
    group_size = tower_count // NGROUP
    piece_rows, width = o_weight.shape
    tokens = attn_out.shape[0]
    piece_cols = width // dp_count
    modal_row = modality.reshape(1, tokens)
    group_ids = jnp.arange(NGROUP, dtype=I32)
    member = modal_row == jnp.arange(KINDS, dtype=I32)[:, None]
    before = jnp.cumsum(member.astype(I32), axis=1) - 1
    order_in = jnp.sum(jnp.where(member, before, 0), axis=0)
    group_of = (group_modality[:, None] == jnp.arange(KINDS, dtype=I32)[None, :]).astype(I32)
    group_rank = jnp.sum((jnp.cumsum(group_of, axis=0) - group_of) * group_of, axis=1)
    how_many = jnp.sum(member * jnp.sum(group_of, axis=0)[:, None], axis=0)
    target = (order_in + tower_idx) % how_many
    chosen = (group_modality[:, None] == modal_row) & (group_rank[:, None] == target[None, :])
    routed = jnp.sum(chosen.astype(I32) * group_ids[:, None], axis=0)
    place = routed * CAP + order_in // how_many
    one_hot = (place[None, :] == jnp.arange(NGROUP * CAP, dtype=I32)[:, None]).astype(BF16)

    def swap(value):
        return lax.all_to_all(value, TOWER, split_axis=0, concat_axis=0, tiled=True)

    cot_group = jnp.dot(one_hot, out_cot, preferred_element_type=F32).astype(BF16)
    attn_group = jnp.dot(one_hot, attn_out, preferred_element_type=F32).astype(BF16)
    cot_send = jnp.broadcast_to(
        cot_group.reshape(NGROUP, 1, CAP, width), (NGROUP, group_size, CAP, width)
    ).reshape(tower_count, CAP, width)
    attn_send = (
        attn_group.reshape(NGROUP, CAP, group_size, piece_rows)
        .transpose(0, 2, 1, 3)
        .reshape(tower_count, CAP, piece_rows)
    )
    cot_rows = swap(cot_send).reshape(tower_count * CAP, width)
    attn_rows = swap(attn_send).reshape(tower_count * CAP, piece_rows)
    grads = lax.dot_general(
        cot_rows, o_weight, (((1,), (1,)), ((), ())), preferred_element_type=F32
    ).astype(BF16)
    returned = (
        swap(grads.reshape(tower_count, CAP, piece_rows))
        .reshape(NGROUP, group_size, CAP, piece_rows)
        .transpose(0, 2, 1, 3)
        .reshape(NGROUP * CAP, width)
    )
    attn_grad = lax.dot_general(
        one_hot, returned, (((0,), (0,)), ((), ())), preferred_element_type=F32
    ).astype(BF16)
    cot_parts = []
    for flip in range(dp_count):
        part = lax.dynamic_slice_in_dim(cot_rows, (dp_idx ^ flip) * piece_cols, piece_cols, 1)
        cot_parts.append(flip_over(DP, part, flip) if flip else part)
    attn_parts = gather_flips(attn_rows)
    return attn_grad, weight_grad_of([attn_parts[flip] for flip in range(dp_count)], cot_parts)


def per_device(*args):
    if lax.axis_size(TOWER) == NGROUP:
        return small_towers(*args)
    return large_towers(*args)


def solution(mesh):
    return jax.shard_map(
        per_device,
        mesh=mesh,
        in_specs=(
            P((DP, TOWER), None),
            P((DP, TOWER), None),
            P((DP, TOWER)),
            P(),
            P(TOWER, None),
        ),
        out_specs=(P((DP, TOWER), None), P(TOWER, DP)),
        check_vma=False,
    )
```
